32 devices in a mesh: bx: 4 (over y, x), by: 8 (over z, core).
Axes of the slice: x: 2, y: 2, z: 4, core: 2. Of those that a mesh axis runs over, the one named last changes fastest.
Arguments:
- cells_in: float32 [128, 5, 4096], P(('bx', 'by')), may hold values from -0.5 to 2, as said below
- block_levels: int32 [128], P(('bx', 'by')), may hold values from 0 to 2
- send_x: int32 [32, 1], P(('bx', 'by')), may hold values from 0 to 3, as said below
- send_y: int32 [32, 1], P(('bx', 'by')), may hold values from 0 to 3, as said below
- layout: int32 [32, 3], P(('bx', 'by')), may hold values from -1 to 5, as said below
- face_out: int32 [32, 4, 4], P(('bx', 'by')), may hold values from 0 to 23, as said below
- ghost_src: int32 [32, 4, 6], P(('bx', 'by')), may hold values from 0 to 39
Outputs:
- cells_out: float32 [96, 5, 4096], P(('bx', 'by'))
The draws below stay inside these ranges and needn't reach their ends.
Inputs may be any that keep to these rules, and one draw needn't show every extreme that they name: `cells_in`: fields 0 and 4 (density, pressure) lie in 1 to 2, fields 1 to 3 (velocities) in -0.5 to 0.5. Per device, send_x and send_y together name 2 distinct slots. Per device, send_x and send_y together name 2 distinct slots. `layout`: each device's codes name each of 4 to 5 once, at most 1 distinct own slots that neither send list names, and -1 for empty slots; some device keeps 1 own slots and some keeps none. `face_out`: entries are face numbers slot * 6 + face of the sending device, distinct within one device and direction.
All inputs are finite; a program needn't handle non-finite values.
Results may differ from the reference program's by a relative error of at most 0.0003.
Values sent between devices are 32-bit elements; how exact they have to be, the bound alone decides.
A program may use at most 64 MiB of HBM per device.

```python
import jax
import jax.numpy as jnp
from jax import lax

B = 16
CAP_IN = 4
MOVE = 1
CAP_OUT = 3
GMAX = 4
BLOCKS_IN = 128
N_BX = 4
N_BY = 8


def draw_cells_in(key, part):
    lower_ends = jnp.array([1.0, -0.5, -0.5, -0.5, 1.0], jnp.float32)[None, :, None]
    upper_ends = jnp.array([2.0, 0.5, 0.5, 0.5, 2.0], jnp.float32)[None, :, None]
    rough = jax.random.uniform(key, (BLOCKS_IN, 5, B * B * B), jnp.float32)
    mixed = rough
    return lower_ends + (upper_ends - lower_ends) * mixed


def migration_lists(key):
    devices = BLOCKS_IN // CAP_IN
    keys_all = jax.random.split(jax.random.fold_in(key, 101), 4)
    perms = jax.vmap(lambda one_key: jax.random.permutation(one_key, CAP_IN))(jax.random.split(keys_all[0], devices)).astype(jnp.int32)
    sent_x = perms[:, :MOVE]
    sent_y = perms[:, MOVE:2 * MOVE]
    spare = perms[:, 2 * MOVE:3 * MOVE]
    device_ids = jnp.arange(devices, dtype=jnp.int32)
    kept = jax.random.randint(keys_all[1], (devices,), 0, MOVE + 1).astype(jnp.int32)
    busiest = jax.random.randint(keys_all[2], (), 0, devices).astype(jnp.int32)
    kept = jnp.where(device_ids == busiest, MOVE, kept)
    kept = jnp.where(device_ids == (busiest + 1) % devices, 0, kept)
    received = jnp.broadcast_to(CAP_IN + jnp.arange(2 * MOVE, dtype=jnp.int32)[None, :], (devices, 2 * MOVE))
    kept_codes = jnp.where(jnp.arange(MOVE, dtype=jnp.int32)[None, :] < kept[:, None], spare, -1)
    slot_codes = jnp.concatenate([received, kept_codes], axis=1)
    orders = jax.vmap(lambda one_key: jax.random.permutation(one_key, CAP_OUT))(jax.random.split(keys_all[3], devices)).astype(jnp.int32)
    placed = jnp.take_along_axis(slot_codes, orders, axis=1).astype(jnp.int32)
    return (sent_x, sent_y, placed)


def draw_send_x(key, part):
    return migration_lists(key)[0]


def draw_send_y(key, part):
    return migration_lists(key)[1]


def draw_layout(key, part):
    return migration_lists(key)[2]


def draw_face_out(key, part):
    devices = BLOCKS_IN // CAP_IN
    perms = jax.vmap(lambda one_key: jax.random.permutation(one_key, 6 * CAP_IN))(jax.random.split(jax.random.fold_in(key, 202), devices * 4))
    return perms[:, :GMAX].reshape(devices, 4, GMAX).astype(jnp.int32)


def draw_ghost_src(key, part):
    devices = BLOCKS_IN // CAP_IN
    keys_all = jax.random.split(jax.random.fold_in(key, 303), 4)
    shape = (devices, CAP_IN, 6)
    chooser = jax.random.randint(keys_all[0], shape, 0, 3)
    local_face = jax.random.randint(keys_all[1], shape, 0, 6 * CAP_IN)
    direction = jax.random.randint(keys_all[2], shape, 0, 4)
    position = jax.random.randint(keys_all[3], shape, 0, GMAX)
    return jnp.where(chooser == 0, local_face, 6 * CAP_IN + direction * GMAX + position).astype(jnp.int32)


def set_ends(entries, rng, smallest, top_value):
    longest = entries.shape.index(max(entries.shape))
    spots = []
    for shift in (0, 1):
        where = [jax.random.randint(jax.random.fold_in(rng, axis), (), 0, length) for axis, length in enumerate(entries.shape)]
        where[longest] = (where[longest] + shift) % entries.shape[longest]
        spots.append(tuple(where))
    return entries.at[spots[0]].set(smallest).at[spots[1]].set(top_value)


def setup_inputs(seed: int = 0) -> dict:
    seeds = jax.random.split(jax.random.key(seed), 8)
    return {
        "cells_in": draw_cells_in(jax.random.fold_in(seeds[7], 71), 0),
        "block_levels": set_ends(jax.random.randint(seeds[1], (BLOCKS_IN,), 0, 3), jax.random.fold_in(seeds[1], 1), 0, 2).astype(jnp.int32),
        "send_x": draw_send_x(jax.random.fold_in(seeds[7], 71), 0),
        "send_y": draw_send_y(jax.random.fold_in(seeds[7], 71), 0),
        "layout": draw_layout(jax.random.fold_in(seeds[7], 71), 0),
        "face_out": draw_face_out(jax.random.fold_in(seeds[7], 71), 0),
        "ghost_src": draw_ghost_src(jax.random.fold_in(seeds[7], 71), 0),
    }


gamma_gas = 1.4
step_base = 0.05

def face_table(blocks):
    number = blocks.shape[0]
    cube_cells = blocks.reshape(number, 5, B, B, B)
    layer_pairs = [(cube_cells[:, :, 0], cube_cells[:, :, 1]), (cube_cells[:, :, B - 1], cube_cells[:, :, B - 2]), (cube_cells[:, :, :, 0], cube_cells[:, :, :, 1]), (cube_cells[:, :, :, B - 1], cube_cells[:, :, :, B - 2]), (cube_cells[:, :, :, :, 0], cube_cells[:, :, :, :, 1]), (cube_cells[:, :, :, :, B - 1], cube_cells[:, :, :, :, B - 2])]
    face_set = jnp.stack([jnp.stack(layer_pair, axis=2) for layer_pair in layer_pairs], axis=1)
    return face_set.reshape(number * 6, 5, 2 * B * B)

def minmod_slope(left_diff, right_diff):
    return 0.5 * (jnp.sign(left_diff) + jnp.sign(right_diff)) * jnp.minimum(jnp.abs(left_diff), jnp.abs(right_diff))

def euler_flux(states, normal):
    density = states[0]
    pressure = states[4]
    normal_vel = states[normal]
    kinetic = 0.5 * density * (states[1] * states[1] + states[2] * states[2] + states[3] * states[3])
    energy = pressure / (gamma_gas - 1.0) + kinetic
    cons_rows = [density] + [density * states[column] for column in range(1, 4)] + [energy]
    flux_rows = [density * normal_vel]
    for column in range(1, 4):
        update_term = density * states[column] * normal_vel
        if column == normal:
            update_term = update_term + pressure
        flux_rows.append(update_term)
    flux_rows.append(normal_vel * (energy + pressure))
    signal = jnp.abs(normal_vel) + jnp.sqrt(gamma_gas * pressure / density)
    return (jnp.stack(flux_rows), jnp.stack(cons_rows), signal)

def sweep(extended, normal, ratio_dt):
    length = extended.shape[1] - 4
    deltas = extended[:, 1:] - extended[:, :-1]
    slopes = minmod_slope(deltas[:, :-1], deltas[:, 1:])
    centre = extended[:, 1:length + 3]
    density = centre[0]
    normal_vel = centre[normal]
    pressure = centre[4]
    advance = [-(normal_vel * slopes[0] + density * slopes[normal])]
    for column in range(1, 4):
        update_term = normal_vel * slopes[column]
        if column == normal:
            update_term = update_term + slopes[4] / density
        advance.append(-update_term)
    advance.append(-(normal_vel * slopes[4] + gamma_gas * pressure * slopes[normal]))
    half_step = 0.5 * ratio_dt * jnp.stack(advance)
    lower_face = centre - 0.5 * slopes + half_step
    upper_face = centre + 0.5 * slopes + half_step
    left_flux, left_cons, left_signal = euler_flux(upper_face[:, :length + 1], normal)
    right_flux, right_cons, right_signal = euler_flux(lower_face[:, 1:length + 2], normal)
    face_flux = 0.5 * (left_flux + right_flux) - 0.5 * jnp.maximum(left_signal, right_signal) * (right_cons - left_cons)
    return face_flux[:, 1:] - face_flux[:, :-1]

def extend_cells(interior, low_side, high_side):
    return jnp.concatenate([low_side[:, 1:2], low_side[:, 0:1], interior, high_side[:, 0:1], high_side[:, 1:2]], axis=1)

def update_block(cells, ghosts, ratio_dt):
    cube_cells = cells.reshape(5, B, B, B)
    ghost_cube = ghosts.reshape(6, 5, 2, B, B)
    along_x = extend_cells(cube_cells, ghost_cube[0], ghost_cube[1]).reshape(5, B + 4, B * B)
    along_y = extend_cells(cube_cells.transpose(0, 2, 1, 3), ghost_cube[2], ghost_cube[3]).reshape(5, B + 4, B * B)
    along_z = extend_cells(cube_cells.transpose(0, 3, 1, 2), ghost_cube[4], ghost_cube[5]).reshape(5, B + 4, B * B)
    change_x = sweep(along_x, 1, ratio_dt).reshape(5, B, B, B)
    change_y = sweep(along_y, 2, ratio_dt).reshape(5, B, B, B).transpose(0, 2, 1, 3)
    change_z = sweep(along_z, 3, ratio_dt).reshape(5, B, B, B).transpose(0, 2, 3, 1)
    flat = cube_cells.reshape(5, B * B * B)
    density = flat[0]
    kinetic = 0.5 * density * (flat[1] * flat[1] + flat[2] * flat[2] + flat[3] * flat[3])
    initial = jnp.stack([density, density * flat[1], density * flat[2], density * flat[3], flat[4] / (gamma_gas - 1.0) + kinetic])
    total = (change_x + change_y + change_z).reshape(5, B * B * B)
    return initial - ratio_dt * total

def reference(cells_in, block_levels, send_x, send_y, layout, face_out, ghost_src):
    devices = N_BX * N_BY
    per_device = 6 * CAP_IN
    device_ids = jnp.arange(devices, dtype=jnp.int32)
    row_index = device_ids // N_BY
    col_index = device_ids % N_BY
    neighbours = jnp.stack([(row_index - 1) % N_BX * N_BY + col_index, (row_index + 1) % N_BX * N_BY + col_index, row_index * N_BY + (col_index - 1) % N_BY, row_index * N_BY + (col_index + 1) % N_BY], axis=1).astype(jnp.int32)
    remote = jnp.maximum(ghost_src - per_device, 0)
    direction = jnp.minimum(remote // GMAX, 3)
    position = remote % GMAX
    sender = neighbours[device_ids[:, None, None], direction]
    remote_face = sender * per_device + face_out[sender, direction, position]
    local_face = device_ids[:, None, None] * per_device + ghost_src
    face_ids = jnp.where(ghost_src < per_device, local_face, remote_face).astype(jnp.int32).reshape(devices * CAP_IN, 6)
    flip_x = N_BX // 2 * N_BY
    flip_y = N_BY // 2
    partner_x = jnp.where(row_index >= N_BX // 2, device_ids - flip_x, device_ids + flip_x).astype(jnp.int32)
    partner_y = jnp.where(col_index >= N_BY // 2, device_ids - flip_y, device_ids + flip_y).astype(jnp.int32)
    own_block = device_ids[:, None] * CAP_IN + jnp.clip(layout, 0, CAP_IN - 1)
    from_x = partner_x[:, None] * CAP_IN + send_x[partner_x[:, None], jnp.clip(layout - CAP_IN, 0, MOVE - 1)]
    from_y = partner_y[:, None] * CAP_IN + send_y[partner_y[:, None], jnp.clip(layout - CAP_IN - MOVE, 0, MOVE - 1)]
    source = jnp.where(layout < CAP_IN, own_block, jnp.where(layout < CAP_IN + MOVE, from_x, from_y)).astype(jnp.int32).reshape(-1)
    filled = layout.reshape(-1) >= 0
    step_sizes = step_base * jnp.exp2(block_levels.astype(jnp.float32))

    def update_one(position_now):
        face_row = face_ids[position_now]
        ghost_list = []
        for face_slot in range(6):
            face_id = face_row[face_slot]
            ghost_list.append(face_table(cells_in[face_id // 6][None])[face_id % 6])
        return update_block(cells_in[position_now], jnp.stack(ghost_list), step_sizes[position_now])
    updated = lax.map(update_one, source)
    return jnp.where(filled[:, None, None], updated, jnp.zeros_like(updated))
```

```python
import functools

import jax
import jax.numpy as jnp
from jax import lax
from jax.experimental import pallas as pl
from jax.experimental.pallas import tpu as pltpu
from jax.sharding import PartitionSpec as P

B = 16
FIELDS = 5
LANES = 128
HALVES = B * B // LANES
STRETCH = (B + 4) * 8
PLANE = 8
FACE = FIELDS * 2 * HALVES
FACE_ROOM = -(-FACE // 8) * 8
ROWS = B * B * B // LANES
BLOCK = FIELDS * ROWS
INNER = B - 4
MESH = pl.DeviceIdType.MESH

SWAPS = (
    (20, ((14, 4), (30, 4), (46, 4), (62, 4), (78, 4), (94, 12))),
    (60, ((106, 8),)),
    (68, ((114, 8),)),
    (76, ((122, 8),)),
)

gamma_gas = 1.4
step_base = 0.05


def choose(mask, a, b):
    if a is None and b is None:
        return None
    return jnp.where(mask, 0.0 if a is None else a, 0.0 if b is None else b)


def roll(value, shift, axis):
    size = (8, LANES)[axis]
    if value is None or shift % size == 0:
        return value
    return pltpu.roll(value, shift % size, axis)


def swap_lanes(planes, unit, lane):
    count = len(planes)
    planes = [roll(p, n * unit, 1) for n, p in enumerate(planes)]
    planes = [planes[-n % count] for n in range(count)]
    step = 1
    while step < count:
        mask = (lane & (step * unit)) != 0
        planes = [choose(mask, planes[(n - step) % count], planes[n]) for n in range(count)]
        step *= 2
    return [roll(p, -n * unit, 1) for n, p in enumerate(planes)]


def swap_xy(planes, coords):
    high = coords[0] >= PLANE // HALVES
    count = len(planes) // HALVES
    first = swap_lanes(planes[:count], B, coords[1])
    second = swap_lanes(planes[count:], B, coords[1])
    moved = [roll(choose(high, a, c), PLANE // HALVES, 0) for a, c in zip(first, second)]
    first = [choose(high, m, a) for m, a in zip(moved, first)]
    second = [choose(high, c, m) for m, c in zip(moved, second)]
    return first + second


def swap_yz(planes, coords):
    return swap_lanes(planes, 1, coords[1])


def plus(a, b):
    return b if a is None else a if b is None else a + b


def minmod(a, b):
    return jnp.maximum(jnp.minimum(a, b), 0.0) + jnp.minimum(jnp.maximum(a, b), 0.0)


def face_values(before, centre, after, half_ratio):
    s = [minmod(c - b, a - c) for b, c, a in zip(before, centre, after)]
    rho, un, _, _, p = centre
    advance = [
        un * s[0] + rho * s[1],
        un * s[1] + s[4] / rho,
        un * s[2],
        un * s[3],
        un * s[4] + gamma_gas * p * s[1],
    ]
    middle = [c - half_ratio * a for c, a in zip(centre, advance)]
    half = [0.5 * v for v in s]
    lower = [m - h for m, h in zip(middle, half)]
    upper = [m + h for m, h in zip(middle, half)]
    return lower, upper


def conserved(state):
    rho, un, u1, u2, p = state
    mn, m1, m2 = rho * un, rho * u1, rho * u2
    energy = p * (1.0 / (gamma_gas - 1.0)) + 0.5 * (mn * un + m1 * u1 + m2 * u2)
    return [rho, mn, m1, m2, energy]


def euler(state):
    rho, un, u1, u2, p = state
    cons = conserved(state)
    mn, energy = cons[1], cons[4]
    flux = [mn, mn * un + p, mn * u1, mn * u2, un * (energy + p)]
    elastic = gamma_gas * p
    signal = jnp.abs(un) + elastic * lax.rsqrt(elastic * rho)
    return flux, cons, signal


def face_flux(left, right):
    fa, ua, sa = euler(left)
    fb, ub, sb = euler(right)
    half_speed = 0.5 * jnp.maximum(sa, sb)
    return [0.5 * (f + g) - half_speed * (v - u) for f, g, u, v in zip(fa, fb, ua, ub)]


def kernel(
    slots, gmax, moves, cap_out,
    cells, levels_in, send_x_in, send_y_in, layout_in, face_out_in, ghost_src_in,
    out,
    edge, local_faces, far_faces, send_faces, ghosts, ext, flux, total,
    early_out, early_in, late_out, late_in, arrived,
    levels, send_x, send_y, layout, face_out, ghost_src,
    face_send, face_recv, early_send, early_recv, late_send, late_recv, cell_sem, small_sem,
):
    cell_copies = [
        pltpu.make_async_copy(
            cells.at[f], ext.at[pl.ds(f * STRETCH + 2 * PLANE, B * PLANE)], cell_sem.at[f]
        )
        for f in range(FIELDS)
    ]
    small = (
        (face_out_in, face_out), (levels_in, levels), (ghost_src_in, ghost_src),
        (send_x_in, send_x), (send_y_in, send_y), (layout_in, layout),
    )
    small_copies = [
        pltpu.make_async_copy(source, target, small_sem.at[i])
        for i, (source, target) in enumerate(small)
    ]
    for copy in cell_copies + small_copies:
        copy.start()
    n_x, n_y = lax.axis_size("bx"), lax.axis_size("by")
    i_x, i_y = lax.axis_index("bx"), lax.axis_index("by")
    beside = (
        {"bx": lax.rem(i_x + 1, n_x)},
        {"bx": lax.rem(i_x + n_x - 1, n_x)},
        {"by": lax.rem(i_y + 1, n_y)},
        {"by": lax.rem(i_y + n_y - 1, n_y)},
    )
    partners = (
        {"bx": lax.rem(i_x + n_x // 2, n_x)},
        {"by": lax.rem(i_y + n_y // 2, n_y)},
    )
    barrier = pltpu.get_barrier_semaphore()
    for device in beside + partners:
        pl.semaphore_signal(barrier, inc=1, device_id=device, device_id_type=MESH)

    coords = [lax.broadcasted_iota(jnp.int32, (8, LANES), axis) for axis in (0, 1)]

    def row(plane):
        return pl.ds(plane * PLANE, PLANE)

    def ext_row(axis, field, plane):
        start = (axis * FIELDS + field) * STRETCH + plane * PLANE
        return pl.ds(pl.multiple_of(start, PLANE), PLANE)

    for copy in cell_copies:
        copy.wait()
    rim = (0, 1, B - 2, B - 1)
    for field in range(FIELDS):
        planes = [ext[ext_row(0, field, x + 2), :] for x in range(B)]
        planes = swap_xy(planes, coords)
        for i, y in enumerate(rim):
            edge[row(field * 4 + i), :] = planes[y]
        planes = swap_yz(planes, coords)
        for i, z in enumerate(rim):
            edge[row((FIELDS + field) * 4 + i), :] = planes[z]

    face_lines = local_faces.reshape(6 * slots * FACE_ROOM, LANES)
    for axis in range(3):
        for side in range(2):
            for layer in range(2):
                nth = layer if side == 0 else 3 - layer
                for field in range(FIELDS):
                    for half in range(HALVES):
                        target = (axis * 2 + side) * FACE_ROOM + field * 4 + layer * 2 + half
                        if axis == 0:
                            at = field * STRETCH + (rim[nth] + 2) * PLANE + half * slots
                            value = ext[pl.ds(at, slots), :]
                        else:
                            at = (((axis - 1) * FIELDS + field) * 4 + nth) * PLANE + half * slots
                            value = edge[pl.ds(at, slots), :]
                        face_lines[pl.ds(target, slots, stride=6 * FACE_ROOM), :] = value

    def local_face(code):
        return local_faces[code][:FACE]

    small_copies[0].wait()
    for d in range(4):
        for k in range(gmax):
            send_faces[d, k] = local_face(face_out[0, d, k])

    pl.semaphore_wait(barrier, 6)
    face_copies = [
        pltpu.make_async_remote_copy(
            src_ref=send_faces.at[d],
            dst_ref=far_faces.at[pl.ds(d * gmax, gmax)],
            send_sem=face_send.at[d],
            recv_sem=face_recv.at[d],
            device_id=beside[d],
            device_id_type=MESH,
        )
        for d in range(4)
    ]
    for copy in face_copies:
        copy.start()
    for field in range(FIELDS):
        planes = [ext[ext_row(0, field, x + 2), :] for x in range(B)]
        planes = swap_xy(planes, coords)
        for y in range(B):
            ext[ext_row(1, field, y + 2), :] = planes[y]
        planes = swap_yz(planes, coords)
        for z in range(B):
            ext[ext_row(2, field, z + 2), :] = planes[z]

    for copy in small_copies[1:]:
        copy.wait()
    slot_of = lax.rem(coords[0], slots)
    level = jnp.zeros((8, LANES), jnp.int32)
    for b in range(slots):
        level = jnp.where(slot_of == b, levels[b], level)
    ratio = step_base * jnp.exp2(level.astype(jnp.float32))
    half_ratio = 0.5 * ratio

    def order(axis):
        return (
            0,
            1 + axis,
            1 + lax.rem(axis + 1, 3),
            1 + lax.rem(axis + 2, 3),
            4,
        )

    def sweep(axis, first, last):
        fields = order(axis)
        load = lambda plane: [ext[ext_row(axis, f, plane), :] for f in fields]
        before, centre = load(first - 1), load(first)
        left = None
        for plane in range(first, last + 1):
            after = load(plane + 1)
            lower, upper = face_values(before, centre, after, half_ratio)
            if left is not None:
                for f, value in zip(fields, face_flux(left, lower)):
                    flux[axis, f, row(plane - 2), :] = value
            left = upper
            before, centre = centre, after

    def inner(axis, carry):
        sweep(axis, 3, B)
        return carry

    lax.fori_loop(0, 3, inner, 0)

    def change(axis, field, faces):
        values = {i: flux[axis, field, row(i), :] for i in faces}
        after = [values.get(i + 1) for i in range(B)]
        before = [values.get(i) for i in range(B)]
        return [plus(a, None if b is None else -b) for a, b in zip(after, before)]

    def changes(field, faces):
        planes = swap_yz(change(2, field, faces), coords)
        planes = [plus(a, c) for a, c in zip(planes, change(1, field, faces))]
        planes = swap_xy(planes, coords)
        return [plus(a, c) for a, c in zip(planes, change(0, field, faces))]

    def total_row(field, x):
        return row(field * B + x)

    for x in range(B):
        initial = conserved([ext[ext_row(0, f, x + 2), :] for f in range(FIELDS)])
        for field in range(FIELDS):
            total[total_row(field, x), :] = initial[field]
    for field in range(FIELDS):
        planes = changes(field, range(2, B - 1))
        for x in range(B):
            total[total_row(field, x), :] = total[total_row(field, x), :] - ratio * planes[x]

    lane = lax.broadcasted_iota(jnp.int32, (INNER, LANES), 1)

    def any_of(spans):
        found = None
        for start, stop in spans:
            test = (lane >= start) & (lane < stop)
            found = test if found is None else found | test
        return found

    into = [any_of([((a + shift) % LANES, (a + shift) % LANES + n) for a, n in spans]) for shift, spans in SWAPS]
    outof = [
        any_of([span for a, n in spans for span in ((a, min(a + n, LANES)), (0, a + n - LANES)) if span[1] > span[0]])
        for shift, spans in SWAPS
    ]

    def exchanged(kept, other, masks, sign):
        for (shift, _), mask in zip(SWAPS, masks):
            kept = jnp.where(mask, pltpu.roll(other, (sign * shift) % LANES, 1), kept)
        return kept

    def half_lines(slot, field, half):
        return total[pl.ds((field * B + 2) * PLANE + half * slots + slot, INNER, stride=PLANE), :]

    def edge_lines(slot, field, x):
        return total[pl.ds((field * B + x) * PLANE + slot, 2 * HALVES, stride=slots), :]

    lists = [(t, m, listed[0, m]) for t, listed in enumerate((send_x, send_y)) for m in range(moves)]

    def to_partner(t, source, target, send_sem, recv_sem):
        return pltpu.make_async_remote_copy(
            src_ref=source.at[t],
            dst_ref=target.at[t],
            send_sem=send_sem.at[t],
            recv_sem=recv_sem.at[t],
            device_id=partners[t],
            device_id_type=MESH,
        )

    for t, m, slot in lists:
        for field in range(FIELDS):
            first, second = (half_lines(slot, field, half) for half in range(HALVES))
            early_out[t, m, pl.ds(field * INNER, INNER), :] = exchanged(second, first, outof, -1)
    early_copies = [to_partner(t, early_out, early_in, early_send, early_recv) for t in range(2)]
    for copy in reversed(early_copies):
        copy.start()

    for copy in face_copies:
        copy.wait()
    for axis in range(3):
        for side in range(2):
            for b in range(slots):
                code = ghost_src[0, b, axis * 2 + side]
                near = local_face(jnp.minimum(code, 6 * slots - 1))
                far = far_faces[jnp.maximum(code - 6 * slots, 0)]
                ghost = b * 6 + axis * 2 + side
                ghosts[ghost] = jnp.where(code < 6 * slots, near, far)
                for layer in range(2):
                    plane = 1 - layer if side == 0 else B + 2 + layer
                    for half in range(HALVES):
                        start = axis * FIELDS * STRETCH + plane * PLANE + half * slots + b
                        ext[pl.ds(start, FIELDS, stride=STRETCH), :] = ghosts[
                            ghost, pl.ds(layer * 2 + half, FIELDS, stride=4), :
                        ]

    def outer(axis, carry):
        sweep(axis, 1, 3)
        sweep(axis, B, B + 2)
        return carry

    lax.fori_loop(0, 3, outer, 0)

    for field in range(FIELDS):
        planes = changes(field, (0, 1, B - 1, B))
        for x in range(B):
            total[total_row(field, x), :] = total[total_row(field, x), :] - ratio * planes[x]

    for t, m, slot in reversed(lists):
        for field in range(FIELDS):
            first, second = (half_lines(slot, field, half) for half in range(HALVES))
            late_out[t, m, pl.ds(field * INNER, INNER), :] = exchanged(first, second, into, 1)
            for i, x in enumerate((0, B - 2)):
                at = FIELDS * INNER + field * 8 + i * 4
                late_out[t, m, pl.ds(at, 4), :] = edge_lines(slot, field, x)
    to_x, to_y = (to_partner(t, late_out, late_in, late_send, late_recv) for t in range(2))
    yields = i_y >= n_y - n_y // 4

    @pl.when(jnp.logical_not(yields))
    def _():
        to_y.start()
        to_x.start()

    @pl.when(yields)
    def _():
        to_x.start()
        to_x.wait_send()
        to_y.start()

    for t in range(2):
        early_copies[t].wait()
    for t in range(2):
        (to_x, to_y)[t].wait_recv()
        for m in range(moves):
            block = t * moves + m
            for field in range(FIELDS):
                early = early_in[t, m, pl.ds(field * INNER, INNER), :]
                late = late_in[t, m, pl.ds(field * INNER, INNER), :]
                at = field * ROWS + 2 * HALVES
                arrived[block, pl.ds(at, INNER, stride=HALVES), :] = exchanged(late, early, into, 1)
                arrived[block, pl.ds(at + 1, INNER, stride=HALVES), :] = exchanged(early, late, outof, -1)
                for i, x in enumerate((0, B - 2)):
                    at = FIELDS * INNER + field * 8 + i * 4
                    arrived[block, pl.ds(field * ROWS + x * HALVES, 4), :] = late_in[t, m, pl.ds(at, 4), :]

    for j in range(cap_out):
        code = layout[0, j]
        mine = jnp.clip(code, 0, slots - 1)
        theirs = jnp.clip(code - slots, 0, 2 * moves - 1)
        for k in range(0, BLOCK, PLANE):
            own = total[pl.ds(mine + k * slots, PLANE, stride=slots), :]
            value = jnp.where(code < slots, own, arrived[theirs, pl.ds(k, PLANE), :])
            out[pl.ds(k * slots + j, PLANE, stride=slots), :] = jnp.where(code < 0, 0.0, value)

    to_y.wait_send()

    @pl.when(jnp.logical_not(yields))
    def _():
        to_x.wait_send()


def on_device(cells_in, block_levels, send_x, send_y, layout, face_out, ghost_src):
    slots = cells_in.shape[0]
    gmax = face_out.shape[2]
    moves = send_x.shape[1]
    cap_out = layout.shape[1]
    small = (block_levels, send_x, send_y, layout, face_out, ghost_src)
    anywhere = pl.BlockSpec(memory_space=pltpu.HBM)
    lines = cells_in.reshape(slots, FIELDS, ROWS, LANES).transpose(1, 2, 0, 3)
    lines = lines.reshape(FIELDS, ROWS * slots, LANES)
    table = functools.partial(pltpu.VMEM, dtype=jnp.float32)
    out = pl.pallas_call(
        functools.partial(kernel, slots, gmax, moves, cap_out),
        out_shape=pltpu.VMEM((FIELDS * B * PLANE, LANES), jnp.float32),
        in_specs=[anywhere] * 7,
        out_specs=pl.BlockSpec(memory_space=pltpu.VMEM),
        scratch_shapes=[
            table((2 * FIELDS * 4 * PLANE, LANES)),
            table((6 * slots, FACE_ROOM, LANES)),
            table((4 * gmax, FACE, LANES)),
            table((4, gmax, FACE, LANES)),
            table((6 * slots, FACE, LANES)),
            table((3 * FIELDS * STRETCH, LANES)),
            table((3, FIELDS, (B + 1) * PLANE, LANES)),
            table((FIELDS * B * PLANE, LANES)),
            table((2, moves, FIELDS * INNER, LANES)),
            table((2, moves, FIELDS * INNER, LANES)),
            table((2, moves, BLOCK - FIELDS * INNER, LANES)),
            table((2, moves, BLOCK - FIELDS * INNER, LANES)),
            table((2 * moves, BLOCK, LANES)),
            *(pltpu.SMEM(a.shape, jnp.int32) for a in small),
            pltpu.SemaphoreType.DMA((4,)),
            pltpu.SemaphoreType.DMA((4,)),
            pltpu.SemaphoreType.DMA((2,)),
            pltpu.SemaphoreType.DMA((2,)),
            pltpu.SemaphoreType.DMA((2,)),
            pltpu.SemaphoreType.DMA((2,)),
            pltpu.SemaphoreType.DMA((FIELDS,)),
            pltpu.SemaphoreType.DMA((len(small),)),
        ],
        compiler_params=pltpu.CompilerParams(collective_id=0, has_side_effects=True),
        name="section",
    )(lines, *small)
    out = out.reshape(FIELDS, ROWS, slots, LANES).transpose(2, 0, 1, 3)
    return out.reshape(slots, FIELDS, ROWS * LANES)[:cap_out]


def solution(mesh):
    return jax.shard_map(
        on_device,
        mesh=mesh,
        in_specs=(
            P(("bx", "by"), None, None),
            P(("bx", "by")),
            P(("bx", "by"), None),
            P(("bx", "by"), None),
            P(("bx", "by"), None),
            P(("bx", "by"), None, None),
            P(("bx", "by"), None, None),
        ),
        out_specs=P(("bx", "by"), None, None),
        check_vma=False,
    )
```

```python
import functools

import jax
import jax.numpy as jnp
from jax import lax
from jax.experimental import pallas as pl
from jax.experimental.pallas import tpu as pltpu
from jax.sharding import PartitionSpec as P

B = 16
FIELDS = 5
LANES = 128
HALVES = B * B // LANES
STRETCH = (B + 4) * 8
PLANE = 8
FACE = FIELDS * 2 * HALVES
FACE_ROOM = -(-FACE // 8) * 8
ROWS = B * B * B // LANES
BLOCK = FIELDS * ROWS
INNER = B - 4
MESH = pl.DeviceIdType.MESH

SWAPS = (
    (20, ((14, 4), (30, 4), (46, 4), (62, 4), (78, 4), (94, 12))),
    (60, ((106, 8),)),
    (68, ((114, 8),)),
    (76, ((122, 8),)),
)

gamma_gas = 1.4
step_base = 0.05


def choose(mask, a, b):
    if a is None and b is None:
        return None
    return jnp.where(mask, 0.0 if a is None else a, 0.0 if b is None else b)


def roll(value, shift, axis):
    size = (8, LANES)[axis]
    if value is None or shift % size == 0:
        return value
    return pltpu.roll(value, shift % size, axis)


def swap_lanes(planes, unit, lane):
    count = len(planes)
    planes = [roll(p, n * unit, 1) for n, p in enumerate(planes)]
    planes = [planes[-n % count] for n in range(count)]
    step = 1
    while step < count:
        mask = (lane & (step * unit)) != 0
        planes = [choose(mask, planes[(n - step) % count], planes[n]) for n in range(count)]
        step *= 2
    return [roll(p, -n * unit, 1) for n, p in enumerate(planes)]


def swap_xy(planes, coords):
    high = coords[0] >= PLANE // HALVES
    count = len(planes) // HALVES
    first = swap_lanes(planes[:count], B, coords[1])
    second = swap_lanes(planes[count:], B, coords[1])
    moved = [roll(choose(high, a, c), PLANE // HALVES, 0) for a, c in zip(first, second)]
    first = [choose(high, m, a) for m, a in zip(moved, first)]
    second = [choose(high, c, m) for m, c in zip(moved, second)]
    return first + second


def swap_yz(planes, coords):
    return swap_lanes(planes, 1, coords[1])


def plus(a, b):
    return b if a is None else a if b is None else a + b


def minmod(a, b):
    return jnp.maximum(jnp.minimum(a, b), 0.0) + jnp.minimum(jnp.maximum(a, b), 0.0)


def face_values(before, centre, after, half_ratio):
    s = [minmod(c - b, a - c) for b, c, a in zip(before, centre, after)]
    rho, un, _, _, p = centre
    advance = [
        un * s[0] + rho * s[1],
        un * s[1] + s[4] / rho,
        un * s[2],
        un * s[3],
        un * s[4] + gamma_gas * p * s[1],
    ]
    middle = [c - half_ratio * a for c, a in zip(centre, advance)]
    half = [0.5 * v for v in s]
    lower = [m - h for m, h in zip(middle, half)]
    upper = [m + h for m, h in zip(middle, half)]
    return lower, upper


def conserved(state):
    rho, un, u1, u2, p = state
    mn, m1, m2 = rho * un, rho * u1, rho * u2
    energy = p * (1.0 / (gamma_gas - 1.0)) + 0.5 * (mn * un + m1 * u1 + m2 * u2)
    return [rho, mn, m1, m2, energy]


def euler(state):
    rho, un, u1, u2, p = state
    cons = conserved(state)
    mn, energy = cons[1], cons[4]
    flux = [mn, mn * un + p, mn * u1, mn * u2, un * (energy + p)]
    elastic = gamma_gas * p
    signal = jnp.abs(un) + elastic * lax.rsqrt(elastic * rho)
    return flux, cons, signal


def face_flux(left, right):
    fa, ua, sa = euler(left)
    fb, ub, sb = euler(right)
    half_speed = 0.5 * jnp.maximum(sa, sb)
    return [0.5 * (f + g) - half_speed * (v - u) for f, g, u, v in zip(fa, fb, ua, ub)]


def kernel(
    slots, gmax, moves, cap_out,
    cells, levels_in, send_x_in, send_y_in, layout_in, face_out_in, ghost_src_in,
    out,
    edge, local_faces, far_faces, send_faces, ext, flux, total,
    early_out, early_in, late_out, late_in, arrived,
    levels, send_x, send_y, layout, face_out, ghost_src,
    face_send, face_recv, early_send, early_recv, late_send, late_recv, cell_sem, small_sem,
):
    cell_copy = pltpu.make_async_copy(
        cells,
        ext.reshape(3 * FIELDS, STRETCH, LANES).at[pl.ds(0, FIELDS), pl.ds(2 * PLANE, B * PLANE)],
        cell_sem,
    )
    cell_copy.start()
    small = (
        (face_out_in, face_out), (levels_in, levels), (ghost_src_in, ghost_src),
        (send_x_in, send_x), (send_y_in, send_y), (layout_in, layout),
    )
    small_copies = [
        pltpu.make_async_copy(source, target, small_sem.at[i])
        for i, (source, target) in enumerate(small)
    ]
    n_x, n_y = lax.axis_size("bx"), lax.axis_size("by")
    i_x, i_y = lax.axis_index("bx"), lax.axis_index("by")
    beside = (
        {"bx": lax.rem(i_x + 1, n_x)},
        {"bx": lax.rem(i_x + n_x - 1, n_x)},
        {"by": lax.rem(i_y + 1, n_y)},
        {"by": lax.rem(i_y + n_y - 1, n_y)},
    )
    partners = (
        {"bx": lax.rem(i_x + n_x // 2, n_x)},
        {"by": lax.rem(i_y + n_y // 2, n_y)},
    )
    barrier = pltpu.get_barrier_semaphore()
    for device in beside + partners:
        pl.semaphore_signal(barrier, inc=1, device_id=device, device_id_type=MESH)
    for copy in small_copies:
        copy.start()

    coords = [lax.broadcasted_iota(jnp.int32, (8, LANES), axis) for axis in (0, 1)]

    def row(plane):
        return pl.ds(plane * PLANE, PLANE)

    def ext_row(axis, field, plane):
        start = (axis * FIELDS + field) * STRETCH + plane * PLANE
        return pl.ds(pl.multiple_of(start, PLANE), PLANE)

    cell_copy.wait()
    rim = (0, 1, B - 2, B - 1)
    for field in range(FIELDS):
        planes = [ext[ext_row(0, field, x + 2), :] for x in range(B)]
        planes = swap_xy(planes, coords)
        for i, y in enumerate(rim):
            edge[row(field * 4 + i), :] = planes[y]
        planes = swap_yz(planes, coords)
        for i, z in enumerate(rim):
            edge[row((FIELDS + field) * 4 + i), :] = planes[z]

    face_lines = local_faces.reshape(6 * slots * FACE_ROOM, LANES)
    for axis in range(3):
        for side in range(2):
            for layer in range(2):
                nth = layer if side == 0 else 3 - layer
                for field in range(FIELDS):
                    for half in range(HALVES):
                        target = (axis * 2 + side) * FACE_ROOM + field * 4 + layer * 2 + half
                        if axis == 0:
                            at = field * STRETCH + (rim[nth] + 2) * PLANE + half * slots
                            value = ext[pl.ds(at, slots), :]
                        else:
                            at = (((axis - 1) * FIELDS + field) * 4 + nth) * PLANE + half * slots
                            value = edge[pl.ds(at, slots), :]
                        face_lines[pl.ds(target, slots, stride=6 * FACE_ROOM), :] = value

    def local_face(code):
        return local_faces[code][:FACE]

    small_copies[0].wait()
    for d in range(4):
        for k in range(gmax):
            send_faces[d, k] = local_face(face_out[0, d, k])

    pl.semaphore_wait(barrier, 6)
    def to_beside(d, source, target):
        return pltpu.make_async_remote_copy(
            src_ref=source,
            dst_ref=target,
            send_sem=face_send,
            recv_sem=face_recv,
            device_id=beside[d],
            device_id_type=MESH,
        )

    for d in range(4):
        to_beside(d, send_faces.at[d], far_faces.at[d]).start()
    all_faces = to_beside(0, send_faces, far_faces)

    for field in range(FIELDS):
        planes = [ext[ext_row(0, field, x + 2), :] for x in range(B)]
        planes = swap_xy(planes, coords)
        for y in range(B):
            ext[ext_row(1, field, y + 2), :] = planes[y]
        planes = swap_yz(planes, coords)
        for z in range(B):
            ext[ext_row(2, field, z + 2), :] = planes[z]

    for copy in small_copies[1:]:
        copy.wait()
    slot_of = lax.rem(coords[0], slots)
    level = jnp.zeros((8, LANES), jnp.int32)
    for b in range(slots):
        level = jnp.where(slot_of == b, levels[b], level)
    ratio = step_base * jnp.exp2(level.astype(jnp.float32))
    half_ratio = 0.5 * ratio

    def order(axis):
        return (
            0,
            1 + axis,
            1 + (axis + 1) % 3,
            1 + (axis + 2) % 3,
            4,
        )

    def sweep(axis, first, last):
        fields = order(axis)
        load = lambda plane: [ext[ext_row(axis, f, plane), :] for f in fields]
        before, centre = load(first - 1), load(first)
        left = None
        for plane in range(first, last + 1):
            after = load(plane + 1)
            lower, upper = face_values(before, centre, after, half_ratio)
            if left is not None:
                for f, value in zip(fields, face_flux(left, lower)):
                    flux[axis, f, row(plane - 2), :] = value
            left = upper
            before, centre = centre, after

    def inner(axis, carry):
        sweep(axis, 3, B)
        return carry

    lax.fori_loop(0, 3, inner, 0)

    def change(axis, field, faces):
        values = {i: flux[axis, field, row(i), :] for i in faces}
        after = [values.get(i + 1) for i in range(B)]
        before = [values.get(i) for i in range(B)]
        return [plus(a, None if b is None else -b) for a, b in zip(after, before)]

    def changes(field, faces):
        planes = swap_yz(change(2, field, faces), coords)
        planes = [plus(a, c) for a, c in zip(planes, change(1, field, faces))]
        planes = swap_xy(planes, coords)
        return [plus(a, c) for a, c in zip(planes, change(0, field, faces))]

    def total_row(field, x):
        return row(field * B + x)

    for x in range(B):
        initial = conserved([ext[ext_row(0, f, x + 2), :] for f in range(FIELDS)])
        for field in range(FIELDS):
            total[total_row(field, x), :] = initial[field]
    for field in range(FIELDS):
        planes = changes(field, range(2, B - 1))
        for x in range(B):
            total[total_row(field, x), :] = total[total_row(field, x), :] - ratio * planes[x]

    lane = lax.broadcasted_iota(jnp.int32, (INNER, LANES), 1)

    def any_of(spans):
        found = None
        for start, stop in spans:
            test = (lane >= start) & (lane < stop)
            found = test if found is None else found | test
        return found

    into = [any_of([((a + shift) % LANES, (a + shift) % LANES + n) for a, n in spans]) for shift, spans in SWAPS]
    outof = [
        any_of([span for a, n in spans for span in ((a, min(a + n, LANES)), (0, a + n - LANES)) if span[1] > span[0]])
        for shift, spans in SWAPS
    ]

    def exchanged(kept, other, masks, sign):
        for (shift, _), mask in zip(SWAPS, masks):
            kept = jnp.where(mask, pltpu.roll(other, (sign * shift) % LANES, 1), kept)
        return kept

    def half_lines(slot, field, half):
        return total[pl.ds((field * B + 2) * PLANE + half * slots + slot, INNER, stride=PLANE), :]

    def edge_lines(slot, field, x):
        return total[pl.ds((field * B + x) * PLANE + slot, 2 * HALVES, stride=slots), :]

    lists = [(t, m, listed[0, m]) for t, listed in enumerate((send_x, send_y)) for m in range(moves)]

    def to_partner(t, source, target, send_sem, recv_sem):
        return pltpu.make_async_remote_copy(
            src_ref=source,
            dst_ref=target,
            send_sem=send_sem,
            recv_sem=recv_sem,
            device_id=partners[t],
            device_id_type=MESH,
        )

    for t, m, slot in lists:
        for field in range(FIELDS):
            first, second = (half_lines(slot, field, half) for half in range(HALVES))
            early_out[t, m, pl.ds(field * INNER, INNER), :] = exchanged(second, first, outof, -1)
    for t in (1, 0):
        to_partner(t, early_out.at[t], early_in.at[t], early_send, early_recv).start()
    all_early = to_partner(0, early_out, early_in, early_send, early_recv)

    all_faces.wait()
    def put_ghosts(axis):
        for side in range(2):
            for b in range(slots):
                code = ghost_src[0, b, axis * 2 + side]
                near = jnp.minimum(code, 6 * slots - 1)
                far = jnp.maximum(code - 6 * slots, 0)
                d, k = lax.div(far, gmax), lax.rem(far, gmax)
                for layer in range(2):
                    plane = 1 - layer if side == 0 else B + 2 + layer
                    for half in range(HALVES):
                        lines = pl.ds(layer * 2 + half, FIELDS, stride=4)
                        start = axis * FIELDS * STRETCH + plane * PLANE + half * slots + b
                        ext[pl.ds(start, FIELDS, stride=STRETCH), :] = jnp.where(
                            code < 6 * slots, local_faces[near, lines, :], far_faces[d, k, lines, :]
                        )

    for axis in (2, 1, 0):
        put_ghosts(axis)
        sweep(axis, 1, 3)
        sweep(axis, B, B + 2)

    for field in range(FIELDS):
        planes = changes(field, (0, 1, B - 1, B))
        for x in range(B):
            total[total_row(field, x), :] = total[total_row(field, x), :] - ratio * planes[x]

    def fill_late(axis):
        for t, m, slot in lists:
            if t != axis:
                continue
            for field in range(FIELDS):
                first, second = (half_lines(slot, field, half) for half in range(HALVES))
                late_out[t, m, pl.ds(field * INNER, INNER), :] = exchanged(first, second, into, 1)
                for i, x in enumerate((0, B - 2)):
                    at = FIELDS * INNER + field * 8 + i * 4
                    late_out[t, m, pl.ds(at, 4), :] = edge_lines(slot, field, x)

    to_x, to_y = (
        to_partner(t, late_out.at[t], late_in.at[t], late_send.at[t], late_recv.at[t]) for t in range(2)
    )
    yields = i_y >= n_y - n_y // 4
    fill_late(1)

    @pl.when(jnp.logical_not(yields))
    def _():
        to_y.start()

    fill_late(0)
    to_x.start()

    @pl.when(yields)
    def _():
        to_x.wait_send()
        to_y.start()

    all_early.wait()
    for t in range(2):
        (to_x, to_y)[t].wait_recv()
        for m in range(moves):
            block = t * moves + m
            for field in range(FIELDS):
                early = early_in[t, m, pl.ds(field * INNER, INNER), :]
                late = late_in[t, m, pl.ds(field * INNER, INNER), :]
                at = field * ROWS + 2 * HALVES
                arrived[block, pl.ds(at, INNER, stride=HALVES), :] = exchanged(late, early, into, 1)
                arrived[block, pl.ds(at + 1, INNER, stride=HALVES), :] = exchanged(early, late, outof, -1)
                for i, x in enumerate((0, B - 2)):
                    at = FIELDS * INNER + field * 8 + i * 4
                    arrived[block, pl.ds(field * ROWS + x * HALVES, 4), :] = late_in[t, m, pl.ds(at, 4), :]

    for j in range(cap_out):
        code = layout[0, j]
        mine = jnp.clip(code, 0, slots - 1)
        theirs = jnp.clip(code - slots, 0, 2 * moves - 1)
        for k in range(0, BLOCK, PLANE):
            own = total[pl.ds(mine + k * slots, PLANE, stride=slots), :]
            value = jnp.where(code < slots, own, arrived[theirs, pl.ds(k, PLANE), :])
            out[pl.ds(k * slots + j, PLANE, stride=slots), :] = jnp.where(code < 0, 0.0, value)

    to_y.wait_send()

    @pl.when(jnp.logical_not(yields))
    def _():
        to_x.wait_send()


def on_device(cells_in, block_levels, send_x, send_y, layout, face_out, ghost_src):
    slots = cells_in.shape[0]
    gmax = face_out.shape[2]
    moves = send_x.shape[1]
    cap_out = layout.shape[1]
    small = (block_levels, send_x, send_y, layout, face_out, ghost_src)
    anywhere = pl.BlockSpec(memory_space=pltpu.HBM)
    lines = cells_in.reshape(slots, FIELDS, ROWS, LANES).transpose(1, 2, 0, 3)
    lines = lines.reshape(FIELDS, ROWS * slots, LANES)
    table = functools.partial(pltpu.VMEM, dtype=jnp.float32)
    out = pl.pallas_call(
        functools.partial(kernel, slots, gmax, moves, cap_out),
        out_shape=pltpu.VMEM((FIELDS * B * PLANE, LANES), jnp.float32),
        in_specs=[anywhere] * 7,
        out_specs=pl.BlockSpec(memory_space=pltpu.VMEM),
        scratch_shapes=[
            table((2 * FIELDS * 4 * PLANE, LANES)),
            table((6 * slots, FACE_ROOM, LANES)),
            table((4, gmax, FACE, LANES)),
            table((4, gmax, FACE, LANES)),
            table((3 * FIELDS * STRETCH, LANES)),
            table((3, FIELDS, (B + 1) * PLANE, LANES)),
            table((FIELDS * B * PLANE, LANES)),
            table((2, moves, FIELDS * INNER, LANES)),
            table((2, moves, FIELDS * INNER, LANES)),
            table((2, moves, BLOCK - FIELDS * INNER, LANES)),
            table((2, moves, BLOCK - FIELDS * INNER, LANES)),
            table((2 * moves, BLOCK, LANES)),
            *(pltpu.SMEM(a.shape, jnp.int32) for a in small),
            pltpu.SemaphoreType.DMA(()),
            pltpu.SemaphoreType.DMA(()),
            pltpu.SemaphoreType.DMA(()),
            pltpu.SemaphoreType.DMA(()),
            pltpu.SemaphoreType.DMA((2,)),
            pltpu.SemaphoreType.DMA((2,)),
            pltpu.SemaphoreType.DMA(()),
            pltpu.SemaphoreType.DMA((len(small),)),
        ],
        compiler_params=pltpu.CompilerParams(collective_id=0, has_side_effects=True),
        name="section",
    )(lines, *small)
    out = out.reshape(FIELDS, ROWS, slots, LANES).transpose(2, 0, 1, 3)
    return out.reshape(slots, FIELDS, ROWS * LANES)[:cap_out]


def solution(mesh):
    return jax.shard_map(
        on_device,
        mesh=mesh,
        in_specs=(
            P(("bx", "by"), None, None),
            P(("bx", "by")),
            P(("bx", "by"), None),
            P(("bx", "by"), None),
            P(("bx", "by"), None),
            P(("bx", "by"), None, None),
            P(("bx", "by"), None, None),
        ),
        out_specs=P(("bx", "by"), None, None),
        check_vma=False,
    )
```

```python
import functools

import jax
import jax.numpy as jnp
from jax import lax
from jax.experimental import pallas as pl
from jax.experimental.pallas import tpu as pltpu
from jax.sharding import PartitionSpec as P

B = 16
FIELDS = 5
LANES = 128
HALVES = B * B // LANES
STRETCH = (B + 4) * 8
PLANE = 8
FACE = FIELDS * 2 * HALVES
FACE_ROOM = -(-FACE // 8) * 8
ROWS = B * B * B // LANES
BLOCK = FIELDS * ROWS
INNER = B - 4
MESH = pl.DeviceIdType.MESH

SWAPS = (
    (20, ((14, 4), (30, 4), (46, 4), (62, 4), (78, 4), (94, 12))),
    (60, ((106, 8),)),
    (68, ((114, 8),)),
    (76, ((122, 8),)),
)

gamma_gas = 1.4
step_base = 0.05


def choose(mask, a, b):
    if a is None and b is None:
        return None
    return jnp.where(mask, 0.0 if a is None else a, 0.0 if b is None else b)


def roll(value, shift, axis):
    size = (8, LANES)[axis]
    if value is None or shift % size == 0:
        return value
    return pltpu.roll(value, shift % size, axis)


def swap_lanes(planes, unit, lane):
    count = len(planes)
    planes = [roll(p, n * unit, 1) for n, p in enumerate(planes)]
    planes = [planes[-n % count] for n in range(count)]
    step = 1
    while step < count:
        mask = (lane & (step * unit)) != 0
        planes = [choose(mask, planes[(n - step) % count], planes[n]) for n in range(count)]
        step *= 2
    return [roll(p, -n * unit, 1) for n, p in enumerate(planes)]


def swap_xy(planes, coords):
    high = coords[0] >= PLANE // HALVES
    count = len(planes) // HALVES
    first = swap_lanes(planes[:count], B, coords[1])
    second = swap_lanes(planes[count:], B, coords[1])
    moved = [roll(choose(high, a, c), PLANE // HALVES, 0) for a, c in zip(first, second)]
    first = [choose(high, m, a) for m, a in zip(moved, first)]
    second = [choose(high, c, m) for m, c in zip(moved, second)]
    return first + second


def swap_yz(planes, coords):
    return swap_lanes(planes, 1, coords[1])


def plus(a, b):
    return b if a is None else a if b is None else a + b


def minmod(a, b):
    return jnp.maximum(jnp.minimum(a, b), 0.0) + jnp.minimum(jnp.maximum(a, b), 0.0)


def face_values(before, centre, after, half_ratio):
    s = [minmod(c - b, a - c) for b, c, a in zip(before, centre, after)]
    rho, un, _, _, p = centre
    advance = [
        un * s[0] + rho * s[1],
        un * s[1] + s[4] / rho,
        un * s[2],
        un * s[3],
        un * s[4] + gamma_gas * p * s[1],
    ]
    middle = [c - half_ratio * a for c, a in zip(centre, advance)]
    half = [0.5 * v for v in s]
    lower = [m - h for m, h in zip(middle, half)]
    upper = [m + h for m, h in zip(middle, half)]
    return lower, upper


def conserved(state):
    rho, un, u1, u2, p = state
    mn, m1, m2 = rho * un, rho * u1, rho * u2
    energy = p * (1.0 / (gamma_gas - 1.0)) + 0.5 * (mn * un + m1 * u1 + m2 * u2)
    return [rho, mn, m1, m2, energy]


def euler(state):
    rho, un, u1, u2, p = state
    cons = conserved(state)
    mn, energy = cons[1], cons[4]
    flux = [mn, mn * un + p, mn * u1, mn * u2, un * (energy + p)]
    elastic = gamma_gas * p
    signal = jnp.abs(un) + elastic * lax.rsqrt(elastic * rho)
    return flux, cons, signal


def face_flux(left, right):
    fa, ua, sa = euler(left)
    fb, ub, sb = euler(right)
    half_speed = 0.5 * jnp.maximum(sa, sb)
    return [0.5 * (f + g) - half_speed * (v - u) for f, g, u, v in zip(fa, fb, ua, ub)]


def kernel(
    slots, gmax, moves, cap_out,
    cells, levels_in, send_x_in, send_y_in, layout_in, face_out_in, ghost_src_in, first_in,
    out,
    edge, local_faces, far_faces, send_faces, ext, flux, total,
    early_out, early_in, late_out, late_in, arrived,
    levels, send_x, send_y, layout, face_out, ghost_src,
    face_send, face_recv, early_send, early_recv, late_send, late_recv, small_sem,
):
    small = (
        (face_out_in, face_out), (levels_in, levels), (ghost_src_in, ghost_src),
        (send_x_in, send_x), (send_y_in, send_y), (layout_in, layout),
    )
    small_copies = [
        pltpu.make_async_copy(source, target, small_sem.at[i])
        for i, (source, target) in enumerate(small)
    ]
    for copy in small_copies:
        copy.start()
    n_x, n_y = lax.axis_size("bx"), lax.axis_size("by")
    i_x, i_y = lax.axis_index("bx"), lax.axis_index("by")
    beside = (
        {"bx": lax.rem(i_x + 1, n_x)},
        {"bx": lax.rem(i_x + n_x - 1, n_x)},
        {"by": lax.rem(i_y + 1, n_y)},
        {"by": lax.rem(i_y + n_y - 1, n_y)},
    )
    partners = (
        {"bx": lax.rem(i_x + n_x // 2, n_x)},
        {"by": lax.rem(i_y + n_y // 2, n_y)},
    )
    barrier = pltpu.get_barrier_semaphore()
    for device in beside + partners:
        pl.semaphore_signal(barrier, inc=1, device_id=device, device_id_type=MESH)

    coords = [lax.broadcasted_iota(jnp.int32, (8, LANES), axis) for axis in (0, 1)]

    def row(plane):
        return pl.ds(plane * PLANE, PLANE)

    def ext_row(axis, field, plane):
        start = (axis * FIELDS + field) * STRETCH + plane * PLANE
        return pl.ds(pl.multiple_of(start, PLANE), PLANE)

    rim = (0, 1, B - 2, B - 1)
    for field in range(FIELDS):
        planes = [cells[field, row(x), :] for x in range(B)]
        for x in range(B):
            ext[ext_row(0, field, x + 2), :] = planes[x]
        planes = swap_xy(planes, coords)
        for i, y in enumerate(rim):
            edge[row(field * 4 + i), :] = planes[y]
        planes = swap_yz(planes, coords)
        for i, z in enumerate(rim):
            edge[row((FIELDS + field) * 4 + i), :] = planes[z]

    face_lines = local_faces.reshape(6 * slots * FACE_ROOM, LANES)
    for axis in range(3):
        for side in range(2):
            for layer in range(2):
                nth = layer if side == 0 else 3 - layer
                for field in range(FIELDS):
                    for half in range(HALVES):
                        target = (axis * 2 + side) * FACE_ROOM + field * 4 + layer * 2 + half
                        if axis == 0:
                            value = cells[field, pl.ds(rim[nth] * PLANE + half * slots, slots), :]
                        else:
                            at = (((axis - 1) * FIELDS + field) * 4 + nth) * PLANE + half * slots
                            value = edge[pl.ds(at, slots), :]
                        face_lines[pl.ds(target, slots, stride=6 * FACE_ROOM), :] = value

    def local_face(code):
        return local_faces[code][:FACE]

    small_copies[0].wait()
    for d in range(4):
        for k in range(gmax):
            send_faces[d, k] = local_face(face_out[0, d, k])

    pl.semaphore_wait(barrier, 6)
    def to_beside(d, source, target):
        return pltpu.make_async_remote_copy(
            src_ref=source,
            dst_ref=target,
            send_sem=face_send,
            recv_sem=face_recv,
            device_id=beside[d],
            device_id_type=MESH,
        )

    for d in range(4):
        to_beside(d, send_faces.at[d], far_faces.at[d]).start()
    all_faces = to_beside(0, send_faces, far_faces)

    for field in range(FIELDS):
        planes = [ext[ext_row(0, field, x + 2), :] for x in range(B)]
        planes = swap_xy(planes, coords)
        for y in range(B):
            ext[ext_row(1, field, y + 2), :] = planes[y]
        planes = swap_yz(planes, coords)
        for z in range(B):
            ext[ext_row(2, field, z + 2), :] = planes[z]

    for copy in small_copies[1:]:
        copy.wait()
    slot_of = lax.rem(coords[0], slots)
    level = jnp.zeros((8, LANES), jnp.int32)
    for b in range(slots):
        level = jnp.where(slot_of == b, levels[b], level)
    ratio = step_base * jnp.exp2(level.astype(jnp.float32))
    half_ratio = 0.5 * ratio

    def order(axis):
        return (
            0,
            1 + axis,
            1 + (axis + 1) % 3,
            1 + (axis + 2) % 3,
            4,
        )

    def sweep(axis, first, last):
        fields = order(axis)
        load = lambda plane: [ext[ext_row(axis, f, plane), :] for f in fields]
        before, centre = load(first - 1), load(first)
        left = None
        for plane in range(first, last + 1):
            after = load(plane + 1)
            lower, upper = face_values(before, centre, after, half_ratio)
            if left is not None:
                for f, value in zip(fields, face_flux(left, lower)):
                    flux[axis, f, row(plane - 2), :] = value
            left = upper
            before, centre = centre, after

    def inner(axis, carry):
        sweep(axis, 3, B)
        return carry

    lax.fori_loop(0, 3, inner, 0)

    def change(axis, field, faces):
        values = {i: flux[axis, field, row(i), :] for i in faces}
        after = [values.get(i + 1) for i in range(B)]
        before = [values.get(i) for i in range(B)]
        return [plus(a, None if b is None else -b) for a, b in zip(after, before)]

    def changes(field, faces):
        planes = swap_yz(change(2, field, faces), coords)
        planes = [plus(a, c) for a, c in zip(planes, change(1, field, faces))]
        planes = swap_xy(planes, coords)
        return [plus(a, c) for a, c in zip(planes, change(0, field, faces))]

    def total_row(field, x):
        return row(field * B + x)

    for x in range(B):
        initial = conserved([ext[ext_row(0, f, x + 2), :] for f in range(FIELDS)])
        for field in range(FIELDS):
            total[total_row(field, x), :] = initial[field]
    for field in range(FIELDS):
        planes = changes(field, range(2, B - 1))
        for x in range(B):
            total[total_row(field, x), :] = total[total_row(field, x), :] - ratio * planes[x]

    lane = lax.broadcasted_iota(jnp.int32, (INNER, LANES), 1)

    def any_of(spans):
        found = None
        for start, stop in spans:
            test = (lane >= start) & (lane < stop)
            found = test if found is None else found | test
        return found

    into = [any_of([((a + shift) % LANES, (a + shift) % LANES + n) for a, n in spans]) for shift, spans in SWAPS]
    outof = [
        any_of([span for a, n in spans for span in ((a, min(a + n, LANES)), (0, a + n - LANES)) if span[1] > span[0]])
        for shift, spans in SWAPS
    ]

    def exchanged(kept, other, masks, sign):
        for (shift, _), mask in zip(SWAPS, masks):
            kept = jnp.where(mask, pltpu.roll(other, (sign * shift) % LANES, 1), kept)
        return kept

    def half_lines(slot, field, half):
        return total[pl.ds((field * B + 2) * PLANE + half * slots + slot, INNER, stride=PLANE), :]

    def edge_lines(slot, field, x):
        return total[pl.ds((field * B + x) * PLANE + slot, 2 * HALVES, stride=slots), :]

    lists = [(t, m, listed[0, m]) for t, listed in enumerate((send_x, send_y)) for m in range(moves)]

    def to_partner(t, source, target, send_sem, recv_sem):
        return pltpu.make_async_remote_copy(
            src_ref=source,
            dst_ref=target,
            send_sem=send_sem,
            recv_sem=recv_sem,
            device_id=partners[t],
            device_id_type=MESH,
        )

    for t, m, slot in lists:
        for field in range(FIELDS):
            first, second = (half_lines(slot, field, half) for half in range(HALVES))
            early_out[t, m, pl.ds(field * INNER, INNER), :] = exchanged(second, first, outof, -1)
    for t in (1, 0):
        to_partner(t, early_out.at[t], early_in.at[t], early_send, early_recv).start()
    all_early = to_partner(0, early_out, early_in, early_send, early_recv)

    all_faces.wait()
    def put_ghosts(axis):
        for side in range(2):
            for b in range(slots):
                code = ghost_src[0, b, axis * 2 + side]
                near = jnp.minimum(code, 6 * slots - 1)
                far = jnp.maximum(code - 6 * slots, 0)
                d, k = lax.div(far, gmax), lax.rem(far, gmax)
                for layer in range(2):
                    plane = 1 - layer if side == 0 else B + 2 + layer
                    for half in range(HALVES):
                        lines = pl.ds(layer * 2 + half, FIELDS, stride=4)
                        start = axis * FIELDS * STRETCH + plane * PLANE + half * slots + b
                        ext[pl.ds(start, FIELDS, stride=STRETCH), :] = jnp.where(
                            code < 6 * slots, local_faces[near, lines, :], far_faces[d, k, lines, :]
                        )

    for axis in (2, 1, 0):
        put_ghosts(axis)
        sweep(axis, 1, 3)
        sweep(axis, B, B + 2)

    for field in range(FIELDS):
        planes = changes(field, (0, 1, B - 1, B))
        for x in range(B):
            total[total_row(field, x), :] = total[total_row(field, x), :] - ratio * planes[x]

    def fill_late(axis):
        for t, m, slot in lists:
            if t != axis:
                continue
            for field in range(FIELDS):
                first, second = (half_lines(slot, field, half) for half in range(HALVES))
                late_out[t, m, pl.ds(field * INNER, INNER), :] = exchanged(first, second, into, 1)
                for i, x in enumerate((0, B - 2)):
                    at = FIELDS * INNER + field * 8 + i * 4
                    late_out[t, m, pl.ds(at, 4), :] = edge_lines(slot, field, x)

    to_x, to_y = (
        to_partner(t, late_out.at[t], late_in.at[t], late_send.at[t], late_recv.at[t]) for t in range(2)
    )
    yields = i_y >= n_y - n_y // 4
    fill_late(1)

    @pl.when(jnp.logical_not(yields))
    def _():
        to_y.start()

    fill_late(0)
    to_x.start()

    @pl.when(yields)
    def _():
        to_x.wait_send()
        to_y.start()

    all_early.wait()
    for t in range(2):
        (to_x, to_y)[t].wait_recv()
        for m in range(moves):
            block = t * moves + m
            for field in range(FIELDS):
                early = early_in[t, m, pl.ds(field * INNER, INNER), :]
                late = late_in[t, m, pl.ds(field * INNER, INNER), :]
                at = field * ROWS + 2 * HALVES
                arrived[block, pl.ds(at, INNER, stride=HALVES), :] = exchanged(late, early, into, 1)
                arrived[block, pl.ds(at + 1, INNER, stride=HALVES), :] = exchanged(early, late, outof, -1)
                for i, x in enumerate((0, B - 2)):
                    at = FIELDS * INNER + field * 8 + i * 4
                    arrived[block, pl.ds(field * ROWS + x * HALVES, 4), :] = late_in[t, m, pl.ds(at, 4), :]

    for j in range(cap_out):
        code = layout[0, j]
        mine = jnp.clip(code, 0, slots - 1)
        theirs = jnp.clip(code - slots, 0, 2 * moves - 1)
        for k in range(0, BLOCK, PLANE):
            own = total[pl.ds(mine + k * slots, PLANE, stride=slots), :]
            value = jnp.where(code < slots, own, arrived[theirs, pl.ds(k, PLANE), :])
            out[pl.ds(k * slots + j, PLANE, stride=slots), :] = jnp.where(code < 0, 0.0, value)

    to_y.wait_send()

    @pl.when(jnp.logical_not(yields))
    def _():
        to_x.wait_send()


def on_device(cells_in, block_levels, send_x, send_y, layout, face_out, ghost_src):
    slots = cells_in.shape[0]
    gmax = face_out.shape[2]
    moves = send_x.shape[1]
    cap_out = layout.shape[1]
    small = (block_levels, send_x, send_y, layout, face_out, ghost_src)
    near = pl.BlockSpec(memory_space=pltpu.VMEM)
    far = pl.BlockSpec(memory_space=pltpu.HBM)
    held = functools.partial(pltpu.with_memory_space_constraint, memory_space=pltpu.VMEM)
    lines = cells_in.reshape(slots, FIELDS, ROWS, LANES).transpose(1, 2, 0, 3)
    lines = lines.reshape(FIELDS, ROWS * slots, LANES)
    table = functools.partial(pltpu.VMEM, dtype=jnp.float32)

    def mark(target):
        target[...] = jnp.zeros_like(target)

    first = pl.pallas_call(
        mark,
        out_shape=pltpu.VMEM((PLANE, LANES), jnp.float32),
        out_specs=near,
        cost_estimate=pl.CostEstimate(flops=100000000, bytes_accessed=0, transcendentals=0),
        name="first",
    )()
    out = pl.pallas_call(
        functools.partial(kernel, slots, gmax, moves, cap_out),
        out_shape=pltpu.VMEM((FIELDS * B * PLANE, LANES), jnp.float32),
        in_specs=[near, *[far] * 6, near],
        out_specs=near,
        scratch_shapes=[
            table((2 * FIELDS * 4 * PLANE, LANES)),
            table((6 * slots, FACE_ROOM, LANES)),
            table((4, gmax, FACE, LANES)),
            table((4, gmax, FACE, LANES)),
            table((3 * FIELDS * STRETCH, LANES)),
            table((3, FIELDS, (B + 1) * PLANE, LANES)),
            table((FIELDS * B * PLANE, LANES)),
            table((2, moves, FIELDS * INNER, LANES)),
            table((2, moves, FIELDS * INNER, LANES)),
            table((2, moves, BLOCK - FIELDS * INNER, LANES)),
            table((2, moves, BLOCK - FIELDS * INNER, LANES)),
            table((2 * moves, BLOCK, LANES)),
            *(pltpu.SMEM(a.shape, jnp.int32) for a in small),
            pltpu.SemaphoreType.DMA(()),
            pltpu.SemaphoreType.DMA(()),
            pltpu.SemaphoreType.DMA(()),
            pltpu.SemaphoreType.DMA(()),
            pltpu.SemaphoreType.DMA((2,)),
            pltpu.SemaphoreType.DMA((2,)),
            pltpu.SemaphoreType.DMA((len(small),)),
        ],
        compiler_params=pltpu.CompilerParams(collective_id=0, has_side_effects=True),
        name="section",
    )(held(lines), *small, held(first))
    out = out.reshape(FIELDS, ROWS, slots, LANES).transpose(2, 0, 1, 3)
    return out.reshape(slots, FIELDS, ROWS * LANES)[:cap_out]


def solution(mesh):
    return jax.shard_map(
        on_device,
        mesh=mesh,
        in_specs=(
            P(("bx", "by"), None, None),
            P(("bx", "by")),
            P(("bx", "by"), None),
            P(("bx", "by"), None),
            P(("bx", "by"), None),
            P(("bx", "by"), None, None),
            P(("bx", "by"), None, None),
        ),
        out_specs=P(("bx", "by"), None, None),
        check_vma=False,
    )
```

```python
import functools

import jax
import jax.numpy as jnp
from jax import lax
from jax.experimental import pallas as pl
from jax.experimental.pallas import tpu as pltpu
from jax.sharding import PartitionSpec as P

B = 16
FIELDS = 5
LANES = 128
HALVES = B * B // LANES
STRETCH = (B + 4) * 8
PLANE = 8
FACE = FIELDS * 2 * HALVES
FACE_ROOM = -(-FACE // 8) * 8
ROWS = B * B * B // LANES
BLOCK = FIELDS * ROWS
INNER = B - 4
MESH = pl.DeviceIdType.MESH

SWAPS = (
    (20, ((14, 4), (30, 4), (46, 4), (62, 4), (78, 4), (94, 12))),
    (60, ((106, 8),)),
    (68, ((114, 8),)),
    (76, ((122, 8),)),
)

gamma_gas = 1.4
step_base = 0.05


def choose(mask, a, b):
    if a is None and b is None:
        return None
    return jnp.where(mask, 0.0 if a is None else a, 0.0 if b is None else b)


def roll(value, shift, axis):
    size = (8, LANES)[axis]
    if value is None or shift % size == 0:
        return value
    return pltpu.roll(value, shift % size, axis)


def swap_lanes(planes, unit, lane):
    count = len(planes)
    planes = [roll(p, n * unit, 1) for n, p in enumerate(planes)]
    planes = [planes[-n % count] for n in range(count)]
    step = 1
    while step < count:
        mask = (lane & (step * unit)) != 0
        planes = [choose(mask, planes[(n - step) % count], planes[n]) for n in range(count)]
        step *= 2
    return [roll(p, -n * unit, 1) for n, p in enumerate(planes)]


def swap_xy(planes, coords):
    high = coords[0] >= PLANE // HALVES
    count = len(planes) // HALVES
    first = swap_lanes(planes[:count], B, coords[1])
    second = swap_lanes(planes[count:], B, coords[1])
    moved = [roll(choose(high, a, c), PLANE // HALVES, 0) for a, c in zip(first, second)]
    first = [choose(high, m, a) for m, a in zip(moved, first)]
    second = [choose(high, c, m) for m, c in zip(moved, second)]
    return first + second


def swap_yz(planes, coords):
    return swap_lanes(planes, 1, coords[1])


def plus(a, b):
    return b if a is None else a if b is None else a + b


def minmod(a, b):
    return jnp.maximum(jnp.minimum(a, b), 0.0) + jnp.minimum(jnp.maximum(a, b), 0.0)


def face_values(before, centre, after, half_ratio):
    s = [minmod(c - b, a - c) for b, c, a in zip(before, centre, after)]
    rho, un, _, _, p = centre
    advance = [
        un * s[0] + rho * s[1],
        un * s[1] + s[4] / rho,
        un * s[2],
        un * s[3],
        un * s[4] + gamma_gas * p * s[1],
    ]
    middle = [c - half_ratio * a for c, a in zip(centre, advance)]
    half = [0.5 * v for v in s]
    lower = [m - h for m, h in zip(middle, half)]
    upper = [m + h for m, h in zip(middle, half)]
    return lower, upper


def conserved(state):
    rho, un, u1, u2, p = state
    mn, m1, m2 = rho * un, rho * u1, rho * u2
    energy = p * (1.0 / (gamma_gas - 1.0)) + 0.5 * (mn * un + m1 * u1 + m2 * u2)
    return [rho, mn, m1, m2, energy]


def euler(state):
    rho, un, u1, u2, p = state
    cons = conserved(state)
    mn, energy = cons[1], cons[4]
    flux = [mn, mn * un + p, mn * u1, mn * u2, un * (energy + p)]
    elastic = gamma_gas * p
    signal = jnp.abs(un) + elastic * lax.rsqrt(elastic * rho)
    return flux, cons, signal


def face_flux(left, right):
    fa, ua, sa = euler(left)
    fb, ub, sb = euler(right)
    half_speed = 0.5 * jnp.maximum(sa, sb)
    return [0.5 * (f + g) - half_speed * (v - u) for f, g, u, v in zip(fa, fb, ua, ub)]


def kernel(
    slots, gmax, moves, cap_out,
    cells, levels_in, send_x_in, send_y_in, layout_in, face_out_in, ghost_src_in, first_in,
    out,
    edge, local_faces, far_faces, send_faces, ext, flux, total,
    early_out, early_in, late_out, late_in, arrived,
    levels, send_x, send_y, layout, face_out, ghost_src,
    face_send, face_recv, early_send, early_recv, late_send, late_recv, small_sem, ready,
):
    small = (
        (face_out_in, face_out), (levels_in, levels), (ghost_src_in, ghost_src),
        (send_x_in, send_x), (send_y_in, send_y), (layout_in, layout),
    )
    small_copies = [
        pltpu.make_async_copy(source, target, small_sem.at[i])
        for i, (source, target) in enumerate(small)
    ]
    for copy in small_copies:
        copy.start()
    n_x, n_y = lax.axis_size("bx"), lax.axis_size("by")
    i_x, i_y = lax.axis_index("bx"), lax.axis_index("by")
    beside = (
        {"bx": lax.rem(i_x + 1, n_x)},
        {"bx": lax.rem(i_x + n_x - 1, n_x)},
        {"by": lax.rem(i_y + 1, n_y)},
        {"by": lax.rem(i_y + n_y - 1, n_y)},
    )
    partners = (
        {"bx": lax.rem(i_x + n_x // 2, n_x)},
        {"by": lax.rem(i_y + n_y // 2, n_y)},
    )
    barrier = pltpu.get_barrier_semaphore()
    first_row, last_row = i_y == 0, i_y == n_y - 1
    upper = (i_x >= n_x // 2, i_y >= n_y // 2)

    def greet(semaphore, device):
        pl.semaphore_signal(semaphore, inc=1, device_id=device, device_id_type=MESH)

    for device in beside[:2] + beside[3:]:
        greet(barrier, device)

    @pl.when(jnp.logical_not(last_row))
    def _():
        greet(barrier, beside[2])

    for t in range(2):

        @pl.when(jnp.logical_not(upper[t]))
        def _(t=t):
            greet(barrier, partners[t])

    coords = [lax.broadcasted_iota(jnp.int32, (8, LANES), axis) for axis in (0, 1)]

    def row(plane):
        return pl.ds(plane * PLANE, PLANE)

    def ext_row(axis, field, plane):
        start = (axis * FIELDS + field) * STRETCH + plane * PLANE
        return pl.ds(pl.multiple_of(start, PLANE), PLANE)

    rim = (0, 1, B - 2, B - 1)
    for field in range(FIELDS):
        planes = [cells[field, row(x), :] for x in range(B)]
        for x in range(B):
            ext[ext_row(0, field, x + 2), :] = planes[x]
        planes = swap_xy(planes, coords)
        for i, y in enumerate(rim):
            edge[row(field * 4 + i), :] = planes[y]
        planes = swap_yz(planes, coords)
        for i, z in enumerate(rim):
            edge[row((FIELDS + field) * 4 + i), :] = planes[z]

    face_lines = local_faces.reshape(6 * slots * FACE_ROOM, LANES)
    for axis in range(3):
        for side in range(2):
            for layer in range(2):
                nth = layer if side == 0 else 3 - layer
                for field in range(FIELDS):
                    for half in range(HALVES):
                        target = (axis * 2 + side) * FACE_ROOM + field * 4 + layer * 2 + half
                        if axis == 0:
                            value = cells[field, pl.ds(rim[nth] * PLANE + half * slots, slots), :]
                        else:
                            at = (((axis - 1) * FIELDS + field) * 4 + nth) * PLANE + half * slots
                            value = edge[pl.ds(at, slots), :]
                        face_lines[pl.ds(target, slots, stride=6 * FACE_ROOM), :] = value

    def local_face(code):
        return local_faces[code][:FACE]

    small_copies[0].wait()
    for d in range(4):
        for k in range(gmax):
            send_faces[d, k] = local_face(face_out[0, d, k])

    expected = 4 - lax.div(n_y - i_y, n_y) + sum(lax.div(i, n // 2) for i, n in ((i_x, n_x), (i_y, n_y)))
    pl.semaphore_wait(barrier, expected)
    def to_beside(d, source, target):
        return pltpu.make_async_remote_copy(
            src_ref=source,
            dst_ref=target,
            send_sem=face_send,
            recv_sem=face_recv,
            device_id=beside[d],
            device_id_type=MESH,
        )

    def send_face(d):
        to_beside(d, send_faces.at[d], far_faces.at[d]).start()

    for d in range(3):
        send_face(d)

    @pl.when(jnp.logical_not(first_row))
    def _():
        send_face(3)

    @pl.when(last_row)
    def _():
        greet(ready.at[0], beside[2])

    for t in range(2):

        @pl.when(upper[t])
        def _(t=t):
            greet(ready.at[1 + t], partners[t])

    all_faces = to_beside(0, send_faces, far_faces)

    for field in range(FIELDS):
        planes = [ext[ext_row(0, field, x + 2), :] for x in range(B)]
        planes = swap_xy(planes, coords)
        for y in range(B):
            ext[ext_row(1, field, y + 2), :] = planes[y]
        planes = swap_yz(planes, coords)
        for z in range(B):
            ext[ext_row(2, field, z + 2), :] = planes[z]

    for copy in small_copies[1:]:
        copy.wait()
    slot_of = lax.rem(coords[0], slots)
    level = jnp.zeros((8, LANES), jnp.int32)
    for b in range(slots):
        level = jnp.where(slot_of == b, levels[b], level)
    ratio = step_base * jnp.exp2(level.astype(jnp.float32))
    half_ratio = 0.5 * ratio

    def order(axis):
        return (
            0,
            1 + axis,
            1 + (axis + 1) % 3,
            1 + (axis + 2) % 3,
            4,
        )

    def sweep(axis, first, last):
        fields = order(axis)
        load = lambda plane: [ext[ext_row(axis, f, plane), :] for f in fields]
        before, centre = load(first - 1), load(first)
        left = None
        for plane in range(first, last + 1):
            after = load(plane + 1)
            lower, upper = face_values(before, centre, after, half_ratio)
            if left is not None:
                for f, value in zip(fields, face_flux(left, lower)):
                    flux[axis, f, row(plane - 2), :] = value
            left = upper
            before, centre = centre, after

    def inner(axis, carry):
        sweep(axis, 3, B)
        return carry

    lax.fori_loop(0, 3, inner, 0)

    def change(axis, field, faces):
        values = {i: flux[axis, field, row(i), :] for i in faces}
        after = [values.get(i + 1) for i in range(B)]
        before = [values.get(i) for i in range(B)]
        return [plus(a, None if b is None else -b) for a, b in zip(after, before)]

    def changes(field, faces):
        planes = swap_yz(change(2, field, faces), coords)
        planes = [plus(a, c) for a, c in zip(planes, change(1, field, faces))]
        planes = swap_xy(planes, coords)
        return [plus(a, c) for a, c in zip(planes, change(0, field, faces))]

    def total_row(field, x):
        return row(field * B + x)

    for x in range(B):
        initial = conserved([ext[ext_row(0, f, x + 2), :] for f in range(FIELDS)])
        for field in range(FIELDS):
            total[total_row(field, x), :] = initial[field]
    for field in range(FIELDS):
        planes = changes(field, range(2, B - 1))
        for x in range(B):
            total[total_row(field, x), :] = total[total_row(field, x), :] - ratio * planes[x]

    @pl.when(first_row)
    def _():
        pl.semaphore_wait(ready.at[0], 1)
        send_face(3)

    lane = lax.broadcasted_iota(jnp.int32, (INNER, LANES), 1)

    def any_of(spans):
        found = None
        for start, stop in spans:
            test = (lane >= start) & (lane < stop)
            found = test if found is None else found | test
        return found

    into = [any_of([((a + shift) % LANES, (a + shift) % LANES + n) for a, n in spans]) for shift, spans in SWAPS]
    outof = [
        any_of([span for a, n in spans for span in ((a, min(a + n, LANES)), (0, a + n - LANES)) if span[1] > span[0]])
        for shift, spans in SWAPS
    ]

    def exchanged(kept, other, masks, sign):
        for (shift, _), mask in zip(SWAPS, masks):
            kept = jnp.where(mask, pltpu.roll(other, (sign * shift) % LANES, 1), kept)
        return kept

    def half_lines(slot, field, half):
        return total[pl.ds((field * B + 2) * PLANE + half * slots + slot, INNER, stride=PLANE), :]

    def edge_lines(slot, field, x):
        return total[pl.ds((field * B + x) * PLANE + slot, 2 * HALVES, stride=slots), :]

    lists = [(t, m, listed[0, m]) for t, listed in enumerate((send_x, send_y)) for m in range(moves)]

    def to_partner(t, source, target, send_sem, recv_sem):
        return pltpu.make_async_remote_copy(
            src_ref=source,
            dst_ref=target,
            send_sem=send_sem,
            recv_sem=recv_sem,
            device_id=partners[t],
            device_id_type=MESH,
        )

    for t, m, slot in lists:
        for field in range(FIELDS):
            first, second = (half_lines(slot, field, half) for half in range(HALVES))
            early_out[t, m, pl.ds(field * INNER, INNER), :] = exchanged(second, first, outof, -1)
    for t in (1, 0):

        @pl.when(jnp.logical_not(upper[t]))
        def _(t=t):
            pl.semaphore_wait(ready.at[1 + t], 1)

        to_partner(t, early_out.at[t], early_in.at[t], early_send, early_recv).start()
    all_early = to_partner(0, early_out, early_in, early_send, early_recv)

    all_faces.wait()
    def put_ghosts(axis):
        for side in range(2):
            for b in range(slots):
                code = ghost_src[0, b, axis * 2 + side]
                near = jnp.minimum(code, 6 * slots - 1)
                far = jnp.maximum(code - 6 * slots, 0)
                d, k = lax.div(far, gmax), lax.rem(far, gmax)
                for layer in range(2):
                    plane = 1 - layer if side == 0 else B + 2 + layer
                    for half in range(HALVES):
                        lines = pl.ds(layer * 2 + half, FIELDS, stride=4)
                        start = axis * FIELDS * STRETCH + plane * PLANE + half * slots + b
                        ext[pl.ds(start, FIELDS, stride=STRETCH), :] = jnp.where(
                            code < 6 * slots, local_faces[near, lines, :], far_faces[d, k, lines, :]
                        )

    for axis in (2, 1, 0):
        put_ghosts(axis)
        sweep(axis, 1, 3)
        sweep(axis, B, B + 2)

    for field in range(FIELDS):
        planes = changes(field, (0, 1, B - 1, B))
        for x in range(B):
            total[total_row(field, x), :] = total[total_row(field, x), :] - ratio * planes[x]

    def fill_late(axis):
        for t, m, slot in lists:
            if t != axis:
                continue
            for field in range(FIELDS):
                first, second = (half_lines(slot, field, half) for half in range(HALVES))
                late_out[t, m, pl.ds(field * INNER, INNER), :] = exchanged(first, second, into, 1)
                for i, x in enumerate((0, B - 2)):
                    at = FIELDS * INNER + field * 8 + i * 4
                    late_out[t, m, pl.ds(at, 4), :] = edge_lines(slot, field, x)

    to_x, to_y = (
        to_partner(t, late_out.at[t], late_in.at[t], late_send.at[t], late_recv.at[t]) for t in range(2)
    )
    fill_late(1)
    to_y.start()
    fill_late(0)
    to_x.start()
    all_early.wait()
    for t in range(2):
        (to_x, to_y)[t].wait_recv()
        for m in range(moves):
            block = t * moves + m
            for field in range(FIELDS):
                early = early_in[t, m, pl.ds(field * INNER, INNER), :]
                late = late_in[t, m, pl.ds(field * INNER, INNER), :]
                at = field * ROWS + 2 * HALVES
                arrived[block, pl.ds(at, INNER, stride=HALVES), :] = exchanged(late, early, into, 1)
                arrived[block, pl.ds(at + 1, INNER, stride=HALVES), :] = exchanged(early, late, outof, -1)
                for i, x in enumerate((0, B - 2)):
                    at = FIELDS * INNER + field * 8 + i * 4
                    arrived[block, pl.ds(field * ROWS + x * HALVES, 4), :] = late_in[t, m, pl.ds(at, 4), :]

    for j in range(cap_out):
        code = layout[0, j]
        mine = jnp.clip(code, 0, slots - 1)
        theirs = jnp.clip(code - slots, 0, 2 * moves - 1)
        for k in range(0, BLOCK, PLANE):
            own = total[pl.ds(mine + k * slots, PLANE, stride=slots), :]
            value = jnp.where(code < slots, own, arrived[theirs, pl.ds(k, PLANE), :])
            out[pl.ds(k * slots + j, PLANE, stride=slots), :] = jnp.where(code < 0, 0.0, value)

    to_y.wait_send()
    to_x.wait_send()


def on_device(cells_in, block_levels, send_x, send_y, layout, face_out, ghost_src):
    slots = cells_in.shape[0]
    gmax = face_out.shape[2]
    moves = send_x.shape[1]
    cap_out = layout.shape[1]
    small = (block_levels, send_x, send_y, layout, face_out, ghost_src)
    near = pl.BlockSpec(memory_space=pltpu.VMEM)
    far = pl.BlockSpec(memory_space=pltpu.HBM)
    held = functools.partial(pltpu.with_memory_space_constraint, memory_space=pltpu.VMEM)
    lines = cells_in.reshape(slots, FIELDS, ROWS, LANES).transpose(1, 2, 0, 3)
    lines = lines.reshape(FIELDS, ROWS * slots, LANES)
    table = functools.partial(pltpu.VMEM, dtype=jnp.float32)

    def mark(target):
        target[...] = jnp.zeros_like(target)

    first = pl.pallas_call(
        mark,
        out_shape=pltpu.VMEM((PLANE, LANES), jnp.float32),
        out_specs=near,
        cost_estimate=pl.CostEstimate(flops=100000000, bytes_accessed=0, transcendentals=0),
        name="first",
    )()
    out = pl.pallas_call(
        functools.partial(kernel, slots, gmax, moves, cap_out),
        out_shape=pltpu.VMEM((FIELDS * B * PLANE, LANES), jnp.float32),
        in_specs=[near, *[far] * 6, near],
        out_specs=near,
        scratch_shapes=[
            table((2 * FIELDS * 4 * PLANE, LANES)),
            table((6 * slots, FACE_ROOM, LANES)),
            table((4, gmax, FACE, LANES)),
            table((4, gmax, FACE, LANES)),
            table((3 * FIELDS * STRETCH, LANES)),
            table((3, FIELDS, (B + 1) * PLANE, LANES)),
            table((FIELDS * B * PLANE, LANES)),
            table((2, moves, FIELDS * INNER, LANES)),
            table((2, moves, FIELDS * INNER, LANES)),
            table((2, moves, BLOCK - FIELDS * INNER, LANES)),
            table((2, moves, BLOCK - FIELDS * INNER, LANES)),
            table((2 * moves, BLOCK, LANES)),
            *(pltpu.SMEM(a.shape, jnp.int32) for a in small),
            pltpu.SemaphoreType.DMA(()),
            pltpu.SemaphoreType.DMA(()),
            pltpu.SemaphoreType.DMA(()),
            pltpu.SemaphoreType.DMA(()),
            pltpu.SemaphoreType.DMA((2,)),
            pltpu.SemaphoreType.DMA((2,)),
            pltpu.SemaphoreType.DMA((len(small),)),
            pltpu.SemaphoreType.REGULAR((3,)),
        ],
        compiler_params=pltpu.CompilerParams(collective_id=0, has_side_effects=True),
        name="section",
    )(held(lines), *small, held(first))
    out = out.reshape(FIELDS, ROWS, slots, LANES).transpose(2, 0, 1, 3)
    return out.reshape(slots, FIELDS, ROWS * LANES)[:cap_out]


def solution(mesh):
    return jax.shard_map(
        on_device,
        mesh=mesh,
        in_specs=(
            P(("bx", "by"), None, None),
            P(("bx", "by")),
            P(("bx", "by"), None),
            P(("bx", "by"), None),
            P(("bx", "by"), None),
            P(("bx", "by"), None, None),
            P(("bx", "by"), None, None),
        ),
        out_specs=P(("bx", "by"), None, None),
        check_vma=False,
    )
```

```python
import functools

import jax
import jax.numpy as jnp
from jax import lax
from jax.experimental import pallas as pl
from jax.experimental.pallas import tpu as pltpu
from jax.sharding import PartitionSpec as P

B = 16
FIELDS = 5
LANES = 128
HALVES = B * B // LANES
STRETCH = (B + 4) * 8
PLANE = 8
FACE = FIELDS * 2 * HALVES
FACE_ROOM = -(-FACE // 8) * 8
ROWS = B * B * B // LANES
BLOCK = FIELDS * ROWS
INNER = B - 4
MESH = pl.DeviceIdType.MESH

SWAPS = (
    (20, ((14, 4), (30, 4), (46, 4), (62, 4), (78, 4), (94, 12))),
    (60, ((106, 8),)),
    (68, ((114, 8),)),
    (76, ((122, 8),)),
)

gamma_gas = 1.4
step_base = 0.05


def choose(mask, a, b):
    if a is None and b is None:
        return None
    return jnp.where(mask, 0.0 if a is None else a, 0.0 if b is None else b)


def roll(value, shift, axis):
    size = (8, LANES)[axis]
    if value is None or shift % size == 0:
        return value
    return pltpu.roll(value, shift % size, axis)


def swap_lanes(planes, unit, lane):
    count = len(planes)
    planes = [roll(p, n * unit, 1) for n, p in enumerate(planes)]
    planes = [planes[-n % count] for n in range(count)]
    step = 1
    while step < count:
        mask = (lane & (step * unit)) != 0
        planes = [choose(mask, planes[(n - step) % count], planes[n]) for n in range(count)]
        step *= 2
    return [roll(p, -n * unit, 1) for n, p in enumerate(planes)]


def swap_xy(planes, coords):
    high = coords[0] >= PLANE // HALVES
    count = len(planes) // HALVES
    first = swap_lanes(planes[:count], B, coords[1])
    second = swap_lanes(planes[count:], B, coords[1])
    moved = [roll(choose(high, a, c), PLANE // HALVES, 0) for a, c in zip(first, second)]
    first = [choose(high, m, a) for m, a in zip(moved, first)]
    second = [choose(high, c, m) for m, c in zip(moved, second)]
    return first + second


def swap_yz(planes, coords):
    return swap_lanes(planes, 1, coords[1])


def plus(a, b):
    return b if a is None else a if b is None else a + b


def minmod(a, b):
    return jnp.maximum(jnp.minimum(a, b), 0.0) + jnp.minimum(jnp.maximum(a, b), 0.0)


def face_values(before, centre, after, half_ratio):
    s = [minmod(c - b, a - c) for b, c, a in zip(before, centre, after)]
    rho, un, _, _, p = centre
    advance = [
        un * s[0] + rho * s[1],
        un * s[1] + s[4] / rho,
        un * s[2],
        un * s[3],
        un * s[4] + gamma_gas * p * s[1],
    ]
    middle = [c - half_ratio * a for c, a in zip(centre, advance)]
    half = [0.5 * v for v in s]
    lower = [m - h for m, h in zip(middle, half)]
    upper = [m + h for m, h in zip(middle, half)]
    return lower, upper


def conserved(state):
    rho, un, u1, u2, p = state
    mn, m1, m2 = rho * un, rho * u1, rho * u2
    energy = p * (1.0 / (gamma_gas - 1.0)) + 0.5 * (mn * un + m1 * u1 + m2 * u2)
    return [rho, mn, m1, m2, energy]


def euler(state):
    rho, un, u1, u2, p = state
    cons = conserved(state)
    mn, energy = cons[1], cons[4]
    flux = [mn, mn * un + p, mn * u1, mn * u2, un * (energy + p)]
    elastic = gamma_gas * p
    signal = jnp.abs(un) + elastic * lax.rsqrt(elastic * rho)
    return flux, cons, signal


def face_flux(left, right):
    fa, ua, sa = euler(left)
    fb, ub, sb = euler(right)
    half_speed = 0.5 * jnp.maximum(sa, sb)
    return [0.5 * (f + g) - half_speed * (v - u) for f, g, u, v in zip(fa, fb, ua, ub)]


def kernel(
    slots, gmax, moves, cap_out,
    cells, levels_in, send_x_in, send_y_in, layout_in, face_out_in, ghost_src_in, first_in,
    out,
    edge, local_faces, far_faces, send_faces, ext, flux, total,
    early_out, early_in, late_out, late_in, arrived,
    levels, send_x, send_y, layout, face_out, ghost_src,
    face_send, face_recv, early_send, early_recv, late_send, late_recv, small_sem, ready,
):
    small = (
        (face_out_in, face_out), (levels_in, levels), (ghost_src_in, ghost_src),
        (send_x_in, send_x), (send_y_in, send_y), (layout_in, layout),
    )
    small_copies = [
        pltpu.make_async_copy(source, target, small_sem.at[i])
        for i, (source, target) in enumerate(small)
    ]
    for copy in small_copies:
        copy.start()
    n_x, n_y = lax.axis_size("bx"), lax.axis_size("by")
    i_x, i_y = lax.axis_index("bx"), lax.axis_index("by")
    beside = (
        {"bx": lax.rem(i_x + 1, n_x)},
        {"bx": lax.rem(i_x + n_x - 1, n_x)},
        {"by": lax.rem(i_y + 1, n_y)},
        {"by": lax.rem(i_y + n_y - 1, n_y)},
    )
    partners = (
        {"bx": lax.rem(i_x + n_x // 2, n_x)},
        {"by": lax.rem(i_y + n_y // 2, n_y)},
    )
    barrier = pltpu.get_barrier_semaphore()
    first_row, last_row = i_y == 0, i_y == n_y - 1
    upper = (i_x >= n_x // 2, i_y >= n_y // 2)

    def greet(semaphore, device):
        pl.semaphore_signal(semaphore, inc=1, device_id=device, device_id_type=MESH)

    for device in beside[:2] + beside[3:]:
        greet(barrier, device)

    @pl.when(jnp.logical_not(last_row))
    def _():
        greet(barrier, beside[2])

    for t in range(2):

        @pl.when(jnp.logical_not(upper[t]))
        def _(t=t):
            greet(barrier, partners[t])

    coords = [lax.broadcasted_iota(jnp.int32, (8, LANES), axis) for axis in (0, 1)]

    def row(plane):
        return pl.ds(plane * PLANE, PLANE)

    def ext_row(axis, field, plane):
        start = (axis * FIELDS + field) * STRETCH + plane * PLANE
        return pl.ds(pl.multiple_of(start, PLANE), PLANE)

    rim = (0, 1, B - 2, B - 1)
    for field in range(FIELDS):
        planes = [cells[field, row(x), :] for x in range(B)]
        for x in range(B):
            ext[ext_row(0, field, x + 2), :] = planes[x]
        planes = swap_xy(planes, coords)
        for i, y in enumerate(rim):
            edge[row(field * 4 + i), :] = planes[y]
        planes = swap_yz(planes, coords)
        for i, z in enumerate(rim):
            edge[row((FIELDS + field) * 4 + i), :] = planes[z]

    face_lines = local_faces.reshape(6 * slots * FACE_ROOM, LANES)
    for axis in range(3):
        for side in range(2):
            for layer in range(2):
                nth = layer if side == 0 else 3 - layer
                for field in range(FIELDS):
                    for half in range(HALVES):
                        target = (axis * 2 + side) * FACE_ROOM + field * 4 + layer * 2 + half
                        if axis == 0:
                            value = cells[field, pl.ds(rim[nth] * PLANE + half * slots, slots), :]
                        else:
                            at = (((axis - 1) * FIELDS + field) * 4 + nth) * PLANE + half * slots
                            value = edge[pl.ds(at, slots), :]
                        face_lines[pl.ds(target, slots, stride=6 * FACE_ROOM), :] = value

    def local_face(code):
        return local_faces[code][:FACE]

    small_copies[0].wait()
    for d in range(4):
        for k in range(gmax):
            send_faces[d, k] = local_face(face_out[0, d, k])

    expected = 4 - lax.div(n_y - i_y, n_y) + sum(lax.div(i, n // 2) for i, n in ((i_x, n_x), (i_y, n_y)))
    pl.semaphore_wait(barrier, expected)
    def to_beside(d, source, target):
        return pltpu.make_async_remote_copy(
            src_ref=source,
            dst_ref=target,
            send_sem=face_send,
            recv_sem=face_recv,
            device_id=beside[d],
            device_id_type=MESH,
        )

    def send_face(d):
        to_beside(d, send_faces.at[d], far_faces.at[d]).start()

    for d in range(3):
        send_face(d)

    @pl.when(jnp.logical_not(first_row))
    def _():
        send_face(3)

    @pl.when(last_row)
    def _():
        greet(ready.at[0], beside[2])

    for t in range(2):

        @pl.when(upper[t])
        def _(t=t):
            greet(ready.at[1 + t], partners[t])

    all_faces = to_beside(0, send_faces, far_faces)

    for field in range(FIELDS):
        planes = [ext[ext_row(0, field, x + 2), :] for x in range(B)]
        planes = swap_xy(planes, coords)
        for y in range(B):
            ext[ext_row(1, field, y + 2), :] = planes[y]
        planes = swap_yz(planes, coords)
        for z in range(B):
            ext[ext_row(2, field, z + 2), :] = planes[z]

    for copy in small_copies[1:]:
        copy.wait()
    slot_of = lax.rem(coords[0], slots)
    level = jnp.zeros((8, LANES), jnp.int32)
    for b in range(slots):
        level = jnp.where(slot_of == b, levels[b], level)
    ratio = step_base * jnp.exp2(level.astype(jnp.float32))
    half_ratio = 0.5 * ratio

    def order(axis):
        return (
            0,
            1 + axis,
            1 + (axis + 1) % 3,
            1 + (axis + 2) % 3,
            4,
        )

    def sweep(axis, first, last):
        fields = order(axis)
        load = lambda plane: [ext[ext_row(axis, f, plane), :] for f in fields]
        before, centre = load(first - 1), load(first)
        left = None
        for plane in range(first, last + 1):
            after = load(plane + 1)
            lower, upper = face_values(before, centre, after, half_ratio)
            if left is not None:
                for f, value in zip(fields, face_flux(left, lower)):
                    flux[axis, f, row(plane - 2), :] = value
            left = upper
            before, centre = centre, after

    def inner(axis, carry):
        sweep(axis, 3, B)
        return carry

    lax.fori_loop(0, 3, inner, 0)

    def change(axis, field, faces):
        values = {i: flux[axis, field, row(i), :] for i in faces}
        after = [values.get(i + 1) for i in range(B)]
        before = [values.get(i) for i in range(B)]
        return [plus(a, None if b is None else -b) for a, b in zip(after, before)]

    def changes(field, faces):
        planes = swap_yz(change(2, field, faces), coords)
        planes = [plus(a, c) for a, c in zip(planes, change(1, field, faces))]
        planes = swap_xy(planes, coords)
        return [plus(a, c) for a, c in zip(planes, change(0, field, faces))]

    def total_row(field, x):
        return row(field * B + x)

    for x in range(B):
        initial = conserved([ext[ext_row(0, f, x + 2), :] for f in range(FIELDS)])
        for field in range(FIELDS):
            total[total_row(field, x), :] = initial[field]
    for field in range(FIELDS):
        planes = changes(field, range(2, B - 1))
        for x in range(B):
            total[total_row(field, x), :] = total[total_row(field, x), :] - ratio * planes[x]

    @pl.when(first_row)
    def _():
        pl.semaphore_wait(ready.at[0], 1)
        send_face(3)

    lane = lax.broadcasted_iota(jnp.int32, (INNER, LANES), 1)

    def any_of(spans):
        found = None
        for start, stop in spans:
            test = (lane >= start) & (lane < stop)
            found = test if found is None else found | test
        return found

    into = [any_of([((a + shift) % LANES, (a + shift) % LANES + n) for a, n in spans]) for shift, spans in SWAPS]
    outof = [
        any_of([span for a, n in spans for span in ((a, min(a + n, LANES)), (0, a + n - LANES)) if span[1] > span[0]])
        for shift, spans in SWAPS
    ]

    def exchanged(kept, other, masks, sign):
        for (shift, _), mask in zip(SWAPS, masks):
            kept = jnp.where(mask, pltpu.roll(other, (sign * shift) % LANES, 1), kept)
        return kept

    def half_lines(slot, field, half):
        return total[pl.ds((field * B + 2) * PLANE + half * slots + slot, INNER, stride=PLANE), :]

    def edge_lines(slot, field, x):
        return total[pl.ds((field * B + x) * PLANE + slot, 2 * HALVES, stride=slots), :]

    lists = [(t, m, listed[0, m]) for t, listed in enumerate((send_x, send_y)) for m in range(moves)]

    def to_partner(t, source, target, send_sem, recv_sem):
        return pltpu.make_async_remote_copy(
            src_ref=source,
            dst_ref=target,
            send_sem=send_sem,
            recv_sem=recv_sem,
            device_id=partners[t],
            device_id_type=MESH,
        )

    for t, m, slot in lists:
        for field in range(FIELDS):
            first, second = (half_lines(slot, field, half) for half in range(HALVES))
            early_out[t, m, pl.ds(field * INNER, INNER), :] = exchanged(second, first, outof, -1)
    for t in (1, 0):

        @pl.when(jnp.logical_not(upper[t]))
        def _(t=t):
            pl.semaphore_wait(ready.at[1 + t], 1)

        to_partner(t, early_out.at[t], early_in.at[t], early_send, early_recv).start()
    all_early = to_partner(0, early_out, early_in, early_send, early_recv)

    all_faces.wait()
    def put_ghosts(axis):
        for side in range(2):
            for b in range(slots):
                code = ghost_src[0, b, axis * 2 + side]
                near = jnp.minimum(code, 6 * slots - 1)
                far = jnp.maximum(code - 6 * slots, 0)
                d, k = lax.div(far, gmax), lax.rem(far, gmax)
                for layer in range(2):
                    plane = 1 - layer if side == 0 else B + 2 + layer
                    for half in range(HALVES):
                        lines = pl.ds(layer * 2 + half, FIELDS, stride=4)
                        start = axis * FIELDS * STRETCH + plane * PLANE + half * slots + b
                        ext[pl.ds(start, FIELDS, stride=STRETCH), :] = jnp.where(
                            code < 6 * slots, local_faces[near, lines, :], far_faces[d, k, lines, :]
                        )

    for axis in (2, 1, 0):
        put_ghosts(axis)
        sweep(axis, 1, 3)
        sweep(axis, B, B + 2)

    for field in range(FIELDS):
        planes = changes(field, (0, 1, B - 1, B))
        for x in range(B):
            total[total_row(field, x), :] = total[total_row(field, x), :] - ratio * planes[x]

    def fill_late(axis):
        for t, m, slot in lists:
            if t != axis:
                continue
            for field in range(FIELDS):
                first, second = (half_lines(slot, field, half) for half in range(HALVES))
                late_out[t, m, pl.ds(field * INNER, INNER), :] = exchanged(first, second, into, 1)
                for i, x in enumerate((0, B - 2)):
                    at = FIELDS * INNER + field * 8 + i * 4
                    late_out[t, m, pl.ds(at, 4), :] = edge_lines(slot, field, x)

    to_x, to_y = (
        to_partner(t, late_out.at[t], late_in.at[t], late_send.at[t], late_recv.at[t]) for t in range(2)
    )
    fill_late(1)
    to_y.start()
    fill_late(0)
    to_x.start()
    all_early.wait()
    swapped = functools.reduce(jnp.logical_or, into)
    for t in range(2):
        for m in range(moves):
            for field in range(FIELDS):
                early = early_in[t, m, pl.ds(field * INNER, INNER), :]
                at = field * ROWS + 2 * HALVES
                arrived[t * moves + m, pl.ds(at, INNER, stride=HALVES), :] = exchanged(early, early, into, 1)
    for t in range(2):
        (to_x, to_y)[t].wait_recv()
        for m in range(moves):
            block = t * moves + m
            for field in range(FIELDS):
                early = early_in[t, m, pl.ds(field * INNER, INNER), :]
                late = late_in[t, m, pl.ds(field * INNER, INNER), :]
                at = field * ROWS + 2 * HALVES
                ahead = arrived[block, pl.ds(at, INNER, stride=HALVES), :]
                arrived[block, pl.ds(at, INNER, stride=HALVES), :] = jnp.where(swapped, ahead, late)
                arrived[block, pl.ds(at + 1, INNER, stride=HALVES), :] = exchanged(early, late, outof, -1)
                for i, x in enumerate((0, B - 2)):
                    at = FIELDS * INNER + field * 8 + i * 4
                    arrived[block, pl.ds(field * ROWS + x * HALVES, 4), :] = late_in[t, m, pl.ds(at, 4), :]

    for j in range(cap_out):
        code = layout[0, j]
        mine = jnp.clip(code, 0, slots - 1)
        theirs = jnp.clip(code - slots, 0, 2 * moves - 1)
        for k in range(0, BLOCK, PLANE):
            own = total[pl.ds(mine + k * slots, PLANE, stride=slots), :]
            value = jnp.where(code < slots, own, arrived[theirs, pl.ds(k, PLANE), :])
            out[pl.ds(k * slots + j, PLANE, stride=slots), :] = jnp.where(code < 0, 0.0, value)

    to_y.wait_send()
    to_x.wait_send()


def on_device(cells_in, block_levels, send_x, send_y, layout, face_out, ghost_src):
    slots = cells_in.shape[0]
    gmax = face_out.shape[2]
    moves = send_x.shape[1]
    cap_out = layout.shape[1]
    small = (block_levels, send_x, send_y, layout, face_out, ghost_src)
    near = pl.BlockSpec(memory_space=pltpu.VMEM)
    far = pl.BlockSpec(memory_space=pltpu.HBM)
    held = functools.partial(pltpu.with_memory_space_constraint, memory_space=pltpu.VMEM)
    lines = cells_in.reshape(slots, FIELDS, ROWS, LANES).transpose(1, 2, 0, 3)
    lines = lines.reshape(FIELDS, ROWS * slots, LANES)
    table = functools.partial(pltpu.VMEM, dtype=jnp.float32)

    def mark(target):
        target[...] = jnp.zeros_like(target)

    first = pl.pallas_call(
        mark,
        out_shape=pltpu.VMEM((PLANE, LANES), jnp.float32),
        out_specs=near,
        cost_estimate=pl.CostEstimate(flops=100000000, bytes_accessed=0, transcendentals=0),
        name="first",
    )()
    out = pl.pallas_call(
        functools.partial(kernel, slots, gmax, moves, cap_out),
        out_shape=pltpu.VMEM((FIELDS * B * PLANE, LANES), jnp.float32),
        in_specs=[near, *[far] * 6, near],
        out_specs=near,
        scratch_shapes=[
            table((2 * FIELDS * 4 * PLANE, LANES)),
            table((6 * slots, FACE_ROOM, LANES)),
            table((4, gmax, FACE, LANES)),
            table((4, gmax, FACE, LANES)),
            table((3 * FIELDS * STRETCH, LANES)),
            table((3, FIELDS, (B + 1) * PLANE, LANES)),
            table((FIELDS * B * PLANE, LANES)),
            table((2, moves, FIELDS * INNER, LANES)),
            table((2, moves, FIELDS * INNER, LANES)),
            table((2, moves, BLOCK - FIELDS * INNER, LANES)),
            table((2, moves, BLOCK - FIELDS * INNER, LANES)),
            table((2 * moves, BLOCK, LANES)),
            *(pltpu.SMEM(a.shape, jnp.int32) for a in small),
            pltpu.SemaphoreType.DMA(()),
            pltpu.SemaphoreType.DMA(()),
            pltpu.SemaphoreType.DMA(()),
            pltpu.SemaphoreType.DMA(()),
            pltpu.SemaphoreType.DMA((2,)),
            pltpu.SemaphoreType.DMA((2,)),
            pltpu.SemaphoreType.DMA((len(small),)),
            pltpu.SemaphoreType.REGULAR((3,)),
        ],
        compiler_params=pltpu.CompilerParams(collective_id=0, has_side_effects=True),
        name="section",
    )(held(lines), *small, held(first))
    out = out.reshape(FIELDS, ROWS, slots, LANES).transpose(2, 0, 1, 3)
    return out.reshape(slots, FIELDS, ROWS * LANES)[:cap_out]


def solution(mesh):
    return jax.shard_map(
        on_device,
        mesh=mesh,
        in_specs=(
            P(("bx", "by"), None, None),
            P(("bx", "by")),
            P(("bx", "by"), None),
            P(("bx", "by"), None),
            P(("bx", "by"), None),
            P(("bx", "by"), None, None),
            P(("bx", "by"), None, None),
        ),
        out_specs=P(("bx", "by"), None, None),
        check_vma=False,
    )
```

```python
import functools

import jax
import jax.numpy as jnp
from jax import lax
from jax.experimental import pallas as pl
from jax.experimental.pallas import tpu as pltpu
from jax.sharding import PartitionSpec as P

B = 16
FIELDS = 5
LANES = 128
HALVES = B * B // LANES
STRETCH = (B + 4) * 8
PLANE = 8
FACE = FIELDS * 2 * HALVES
FACE_ROOM = -(-FACE // 8) * 8
ROWS = B * B * B // LANES
BLOCK = FIELDS * ROWS
INNER = B - 4
MESH = pl.DeviceIdType.MESH

SWAPS = (
    (20, ((14, 4), (30, 4), (46, 4), (62, 4), (78, 4), (94, 12))),
    (60, ((106, 8),)),
    (68, ((114, 8),)),
    (76, ((122, 8),)),
)

gamma_gas = 1.4
step_base = 0.05


def choose(mask, a, b):
    if a is None and b is None:
        return None
    return jnp.where(mask, 0.0 if a is None else a, 0.0 if b is None else b)


def roll(value, shift, axis):
    size = (8, LANES)[axis]
    if value is None or shift % size == 0:
        return value
    return pltpu.roll(value, shift % size, axis)


def swap_lanes(planes, unit, lane):
    count = len(planes)
    planes = [roll(p, n * unit, 1) for n, p in enumerate(planes)]
    planes = [planes[-n % count] for n in range(count)]
    step = 1
    while step < count:
        mask = (lane & (step * unit)) != 0
        planes = [choose(mask, planes[(n - step) % count], planes[n]) for n in range(count)]
        step *= 2
    return [roll(p, -n * unit, 1) for n, p in enumerate(planes)]


def swap_xy(planes, coords):
    high = coords[0] >= PLANE // HALVES
    count = len(planes) // HALVES
    first = swap_lanes(planes[:count], B, coords[1])
    second = swap_lanes(planes[count:], B, coords[1])
    moved = [roll(choose(high, a, c), PLANE // HALVES, 0) for a, c in zip(first, second)]
    first = [choose(high, m, a) for m, a in zip(moved, first)]
    second = [choose(high, c, m) for m, c in zip(moved, second)]
    return first + second


def swap_yz(planes, coords):
    return swap_lanes(planes, 1, coords[1])


def plus(a, b):
    return b if a is None else a if b is None else a + b


def minmod(a, b):
    return jnp.maximum(jnp.minimum(a, b), 0.0) + jnp.minimum(jnp.maximum(a, b), 0.0)


def face_values(before, centre, after, half_ratio):
    s = [minmod(c - b, a - c) for b, c, a in zip(before, centre, after)]
    rho, un, _, _, p = centre
    advance = [
        un * s[0] + rho * s[1],
        un * s[1] + s[4] / rho,
        un * s[2],
        un * s[3],
        un * s[4] + gamma_gas * p * s[1],
    ]
    middle = [c - half_ratio * a for c, a in zip(centre, advance)]
    half = [0.5 * v for v in s]
    lower = [m - h for m, h in zip(middle, half)]
    upper = [m + h for m, h in zip(middle, half)]
    return lower, upper


def conserved(state):
    rho, un, u1, u2, p = state
    mn, m1, m2 = rho * un, rho * u1, rho * u2
    energy = p * (1.0 / (gamma_gas - 1.0)) + 0.5 * (mn * un + m1 * u1 + m2 * u2)
    return [rho, mn, m1, m2, energy]


def euler(state):
    rho, un, u1, u2, p = state
    cons = conserved(state)
    mn, energy = cons[1], cons[4]
    flux = [mn, mn * un + p, mn * u1, mn * u2, un * (energy + p)]
    elastic = gamma_gas * p
    signal = jnp.abs(un) + elastic * lax.rsqrt(elastic * rho)
    return flux, cons, signal


def face_flux(left, right):
    fa, ua, sa = euler(left)
    fb, ub, sb = euler(right)
    half_speed = 0.5 * jnp.maximum(sa, sb)
    return [0.5 * (f + g) - half_speed * (v - u) for f, g, u, v in zip(fa, fb, ua, ub)]


def kernel(
    slots, gmax, moves, cap_out,
    cells, levels_in, send_x_in, send_y_in, layout_in, face_out_in, ghost_src_in, first_in,
    out,
    edge, local_faces, far_faces, send_faces, ext, flux, total,
    early_out, early_in, late_out, late_in, arrived,
    levels, send_x, send_y, layout, face_out, ghost_src,
    face_send, face_recv, early_send, early_recv, late_send, late_recv, small_sem, ready,
):
    small = (
        (face_out_in, face_out), (levels_in, levels), (ghost_src_in, ghost_src),
        (send_x_in, send_x), (send_y_in, send_y), (layout_in, layout),
    )
    small_copies = [
        pltpu.make_async_copy(source, target, small_sem.at[i])
        for i, (source, target) in enumerate(small)
    ]
    for copy in small_copies:
        copy.start()
    n_x, n_y = lax.axis_size("bx"), lax.axis_size("by")
    i_x, i_y = lax.axis_index("bx"), lax.axis_index("by")
    beside = (
        {"bx": lax.rem(i_x + 1, n_x)},
        {"bx": lax.rem(i_x + n_x - 1, n_x)},
        {"by": lax.rem(i_y + 1, n_y)},
        {"by": lax.rem(i_y + n_y - 1, n_y)},
    )
    partners = (
        {"bx": lax.rem(i_x + n_x // 2, n_x)},
        {"by": lax.rem(i_y + n_y // 2, n_y)},
    )
    barrier = pltpu.get_barrier_semaphore()
    first_row, last_row = i_y == 0, i_y == n_y - 1
    upper = (i_x >= n_x // 2, i_y >= n_y // 2)

    def greet(semaphore, device):
        pl.semaphore_signal(semaphore, inc=1, device_id=device, device_id_type=MESH)

    for device in beside[:2] + beside[3:]:
        greet(barrier, device)

    @pl.when(jnp.logical_not(last_row))
    def _():
        greet(barrier, beside[2])

    for t in range(2):

        @pl.when(jnp.logical_not(upper[t]))
        def _(t=t):
            greet(barrier, partners[t])

    coords = [lax.broadcasted_iota(jnp.int32, (8, LANES), axis) for axis in (0, 1)]

    def row(plane):
        return pl.ds(plane * PLANE, PLANE)

    def ext_row(axis, field, plane):
        start = (axis * FIELDS + field) * STRETCH + plane * PLANE
        return pl.ds(pl.multiple_of(start, PLANE), PLANE)

    rim = (0, 1, B - 2, B - 1)
    for field in range(FIELDS):
        planes = [cells[field, row(x), :] for x in range(B)]
        for x in range(B):
            ext[ext_row(0, field, x + 2), :] = planes[x]
        planes = swap_xy(planes, coords)
        for i, y in enumerate(rim):
            edge[row(field * 4 + i), :] = planes[y]
        planes = swap_yz(planes, coords)
        for i, z in enumerate(rim):
            edge[row((FIELDS + field) * 4 + i), :] = planes[z]

    face_lines = local_faces.reshape(6 * slots * FACE_ROOM, LANES)
    for axis in range(3):
        for side in range(2):
            for layer in range(2):
                nth = layer if side == 0 else 3 - layer
                for field in range(FIELDS):
                    for half in range(HALVES):
                        target = (axis * 2 + side) * FACE_ROOM + field * 4 + layer * 2 + half
                        if axis == 0:
                            value = cells[field, pl.ds(rim[nth] * PLANE + half * slots, slots), :]
                        else:
                            at = (((axis - 1) * FIELDS + field) * 4 + nth) * PLANE + half * slots
                            value = edge[pl.ds(at, slots), :]
                        face_lines[pl.ds(target, slots, stride=6 * FACE_ROOM), :] = value

    def local_face(code):
        return local_faces[code][:FACE]

    small_copies[0].wait()
    for d in range(4):
        for k in range(gmax):
            send_faces[d, k] = local_face(face_out[0, d, k])

    expected = 4 - lax.div(n_y - i_y, n_y) + sum(lax.div(i, n // 2) for i, n in ((i_x, n_x), (i_y, n_y)))
    pl.semaphore_wait(barrier, expected)
    def to_beside(d, source, target):
        return pltpu.make_async_remote_copy(
            src_ref=source,
            dst_ref=target,
            send_sem=face_send,
            recv_sem=face_recv,
            device_id=beside[d],
            device_id_type=MESH,
        )

    def send_face(d):
        to_beside(d, send_faces.at[d], far_faces.at[d]).start()

    for d in range(3):
        send_face(d)

    @pl.when(jnp.logical_not(first_row))
    def _():
        send_face(3)

    @pl.when(last_row)
    def _():
        greet(ready.at[0], beside[2])

    for t in range(2):

        @pl.when(upper[t])
        def _(t=t):
            greet(ready.at[1 + t], partners[t])

    all_faces = to_beside(0, send_faces, far_faces)

    for field in range(FIELDS):
        planes = [ext[ext_row(0, field, x + 2), :] for x in range(B)]
        planes = swap_xy(planes, coords)
        for y in range(B):
            ext[ext_row(1, field, y + 2), :] = planes[y]
        planes = swap_yz(planes, coords)
        for z in range(B):
            ext[ext_row(2, field, z + 2), :] = planes[z]

    for copy in small_copies[1:]:
        copy.wait()
    slot_of = lax.rem(coords[0], slots)
    level = jnp.zeros((8, LANES), jnp.int32)
    for b in range(slots):
        level = jnp.where(slot_of == b, levels[b], level)
    ratio = step_base * jnp.exp2(level.astype(jnp.float32))
    half_ratio = 0.5 * ratio

    def order(axis):
        return (
            0,
            1 + axis,
            1 + (axis + 1) % 3,
            1 + (axis + 2) % 3,
            4,
        )

    def sweep(axis, first, last):
        fields = order(axis)
        load = lambda plane: [ext[ext_row(axis, f, plane), :] for f in fields]
        before, centre = load(first - 1), load(first)
        left = None
        for plane in range(first, last + 1):
            after = load(plane + 1)
            lower, upper = face_values(before, centre, after, half_ratio)
            if left is not None:
                for f, value in zip(fields, face_flux(left, lower)):
                    flux[axis, f, row(plane - 2), :] = value
            left = upper
            before, centre = centre, after

    def inner(axis, carry):
        sweep(axis, 3, B)
        return carry

    lax.fori_loop(0, 3, inner, 0)

    def change(axis, field, faces):
        values = {i: flux[axis, field, row(i), :] for i in faces}
        after = [values.get(i + 1) for i in range(B)]
        before = [values.get(i) for i in range(B)]
        return [plus(a, None if b is None else -b) for a, b in zip(after, before)]

    def changes(field, faces):
        planes = swap_yz(change(2, field, faces), coords)
        planes = [plus(a, c) for a, c in zip(planes, change(1, field, faces))]
        planes = swap_xy(planes, coords)
        return [plus(a, c) for a, c in zip(planes, change(0, field, faces))]

    def total_row(field, x):
        return row(field * B + x)

    for x in range(B):
        initial = conserved([ext[ext_row(0, f, x + 2), :] for f in range(FIELDS)])
        for field in range(FIELDS):
            total[total_row(field, x), :] = initial[field]
    for field in range(FIELDS):
        planes = changes(field, range(2, B - 1))
        for x in range(B):
            total[total_row(field, x), :] = total[total_row(field, x), :] - ratio * planes[x]

    @pl.when(first_row)
    def _():
        pl.semaphore_wait(ready.at[0], 1)
        send_face(3)

    lane = lax.broadcasted_iota(jnp.int32, (INNER, LANES), 1)

    def any_of(spans):
        found = None
        for start, stop in spans:
            test = (lane >= start) & (lane < stop)
            found = test if found is None else found | test
        return found

    into = [any_of([((a + shift) % LANES, (a + shift) % LANES + n) for a, n in spans]) for shift, spans in SWAPS]
    outof = [
        any_of([span for a, n in spans for span in ((a, min(a + n, LANES)), (0, a + n - LANES)) if span[1] > span[0]])
        for shift, spans in SWAPS
    ]

    def exchanged(kept, other, masks, sign):
        for (shift, _), mask in zip(SWAPS, masks):
            kept = jnp.where(mask, pltpu.roll(other, (sign * shift) % LANES, 1), kept)
        return kept

    def half_lines(slot, field, half):
        return total[pl.ds((field * B + 2) * PLANE + half * slots + slot, INNER, stride=PLANE), :]

    def edge_lines(slot, field, x):
        return total[pl.ds((field * B + x) * PLANE + slot, 2 * HALVES, stride=slots), :]

    lists = [(t, m, listed[0, m]) for t, listed in enumerate((send_x, send_y)) for m in range(moves)]

    def to_partner(t, source, target, send_sem, recv_sem):
        return pltpu.make_async_remote_copy(
            src_ref=source,
            dst_ref=target,
            send_sem=send_sem,
            recv_sem=recv_sem,
            device_id=partners[t],
            device_id_type=MESH,
        )

    for t, m, slot in lists:
        for field in range(FIELDS):
            first, second = (half_lines(slot, field, half) for half in range(HALVES))
            early_out[t, m, pl.ds(field * INNER, INNER), :] = exchanged(second, first, outof, -1)
    for t in (1, 0):

        @pl.when(jnp.logical_not(upper[t]))
        def _(t=t):
            pl.semaphore_wait(ready.at[1 + t], 1)

        to_partner(t, early_out.at[t], early_in.at[t], early_send, early_recv).start()
    all_early = to_partner(0, early_out, early_in, early_send, early_recv)

    all_faces.wait()
    def put_ghosts(axis):
        for side in range(2):
            for b in range(slots):
                code = ghost_src[0, b, axis * 2 + side]
                near = jnp.minimum(code, 6 * slots - 1)
                far = jnp.maximum(code - 6 * slots, 0)
                d, k = lax.div(far, gmax), lax.rem(far, gmax)
                for layer in range(2):
                    plane = 1 - layer if side == 0 else B + 2 + layer
                    for half in range(HALVES):
                        lines = pl.ds(layer * 2 + half, FIELDS, stride=4)
                        start = axis * FIELDS * STRETCH + plane * PLANE + half * slots + b
                        ext[pl.ds(start, FIELDS, stride=STRETCH), :] = jnp.where(
                            code < 6 * slots, local_faces[near, lines, :], far_faces[d, k, lines, :]
                        )

    for axis in (2, 1, 0):
        put_ghosts(axis)
        sweep(axis, 1, 3)
        sweep(axis, B, B + 2)

    for field in range(FIELDS):
        planes = changes(field, (0, 1, B - 1, B))
        for x in range(B):
            total[total_row(field, x), :] = total[total_row(field, x), :] - ratio * planes[x]

    def fill_late(axis):
        for t, m, slot in lists:
            if t != axis:
                continue
            for field in range(FIELDS):
                first, second = (half_lines(slot, field, half) for half in range(HALVES))
                late_out[t, m, pl.ds(field * INNER, INNER), :] = exchanged(first, second, into, 1)
                for i, x in enumerate((0, B - 2)):
                    at = FIELDS * INNER + field * 8 + i * 4
                    late_out[t, m, pl.ds(at, 4), :] = edge_lines(slot, field, x)

    to_x, to_y = (
        to_partner(t, late_out.at[t], late_in.at[t], late_send, late_recv.at[t]) for t in range(2)
    )
    fill_late(1)
    to_y.start()
    fill_late(0)
    to_x.start()
    all_early.wait()
    swapped = functools.reduce(jnp.logical_or, into)
    for t in range(2):
        for m in range(moves):
            for field in range(FIELDS):
                early = early_in[t, m, pl.ds(field * INNER, INNER), :]
                at = field * ROWS + 2 * HALVES
                arrived[t * moves + m, pl.ds(at, INNER, stride=HALVES), :] = exchanged(early, early, into, 1)
    for t in range(2):
        (to_x, to_y)[t].wait_recv()
        for m in range(moves):
            block = t * moves + m
            for field in range(FIELDS):
                early = early_in[t, m, pl.ds(field * INNER, INNER), :]
                late = late_in[t, m, pl.ds(field * INNER, INNER), :]
                at = field * ROWS + 2 * HALVES
                ahead = arrived[block, pl.ds(at, INNER, stride=HALVES), :]
                arrived[block, pl.ds(at, INNER, stride=HALVES), :] = jnp.where(swapped, ahead, late)
                arrived[block, pl.ds(at + 1, INNER, stride=HALVES), :] = exchanged(early, late, outof, -1)
                for i, x in enumerate((0, B - 2)):
                    at = FIELDS * INNER + field * 8 + i * 4
                    arrived[block, pl.ds(field * ROWS + x * HALVES, 4), :] = late_in[t, m, pl.ds(at, 4), :]

    for j in range(cap_out):
        code = layout[0, j]
        mine = jnp.clip(code, 0, slots - 1)
        theirs = jnp.clip(code - slots, 0, 2 * moves - 1)
        for k in range(0, BLOCK, PLANE):
            own = total[pl.ds(mine + k * slots, PLANE, stride=slots), :]
            value = jnp.where(code < slots, own, arrived[theirs, pl.ds(k, PLANE), :])
            out[pl.ds(k * slots + j, PLANE, stride=slots), :] = jnp.where(code < 0, 0.0, value)

    to_partner(0, late_out, late_in, late_send, late_recv.at[0]).wait_send()


def on_device(cells_in, block_levels, send_x, send_y, layout, face_out, ghost_src):
    slots = cells_in.shape[0]
    gmax = face_out.shape[2]
    moves = send_x.shape[1]
    cap_out = layout.shape[1]
    small = (block_levels, send_x, send_y, layout, face_out, ghost_src)
    near = pl.BlockSpec(memory_space=pltpu.VMEM)
    far = pl.BlockSpec(memory_space=pltpu.HBM)
    held = functools.partial(pltpu.with_memory_space_constraint, memory_space=pltpu.VMEM)
    lines = cells_in.reshape(slots, FIELDS, ROWS, LANES).transpose(1, 2, 0, 3)
    lines = lines.reshape(FIELDS, ROWS * slots, LANES)
    table = functools.partial(pltpu.VMEM, dtype=jnp.float32)

    def mark(target):
        target[...] = jnp.zeros_like(target)

    first = pl.pallas_call(
        mark,
        out_shape=pltpu.VMEM((PLANE, LANES), jnp.float32),
        out_specs=near,
        cost_estimate=pl.CostEstimate(flops=100000000, bytes_accessed=0, transcendentals=0),
        name="first",
    )()
    out = pl.pallas_call(
        functools.partial(kernel, slots, gmax, moves, cap_out),
        out_shape=pltpu.VMEM((FIELDS * B * PLANE, LANES), jnp.float32),
        in_specs=[near, *[far] * 6, near],
        out_specs=near,
        scratch_shapes=[
            table((2 * FIELDS * 4 * PLANE, LANES)),
            table((6 * slots, FACE_ROOM, LANES)),
            table((4, gmax, FACE, LANES)),
            table((4, gmax, FACE, LANES)),
            table((3 * FIELDS * STRETCH, LANES)),
            table((3, FIELDS, (B + 1) * PLANE, LANES)),
            table((FIELDS * B * PLANE, LANES)),
            table((2, moves, FIELDS * INNER, LANES)),
            table((2, moves, FIELDS * INNER, LANES)),
            table((2, moves, BLOCK - FIELDS * INNER, LANES)),
            table((2, moves, BLOCK - FIELDS * INNER, LANES)),
            table((2 * moves, BLOCK, LANES)),
            *(pltpu.SMEM(a.shape, jnp.int32) for a in small),
            pltpu.SemaphoreType.DMA(()),
            pltpu.SemaphoreType.DMA(()),
            pltpu.SemaphoreType.DMA(()),
            pltpu.SemaphoreType.DMA(()),
            pltpu.SemaphoreType.DMA(()),
            pltpu.SemaphoreType.DMA((2,)),
            pltpu.SemaphoreType.DMA((len(small),)),
            pltpu.SemaphoreType.REGULAR((3,)),
        ],
        compiler_params=pltpu.CompilerParams(collective_id=0, has_side_effects=True),
        name="section",
    )(held(lines), *small, held(first))
    out = out.reshape(FIELDS, ROWS, slots, LANES).transpose(2, 0, 1, 3)
    return out.reshape(slots, FIELDS, ROWS * LANES)[:cap_out]


def solution(mesh):
    return jax.shard_map(
        on_device,
        mesh=mesh,
        in_specs=(
            P(("bx", "by"), None, None),
            P(("bx", "by")),
            P(("bx", "by"), None),
            P(("bx", "by"), None),
            P(("bx", "by"), None),
            P(("bx", "by"), None, None),
            P(("bx", "by"), None, None),
        ),
        out_specs=P(("bx", "by"), None, None),
        check_vma=False,
    )
```
